32 devices in a mesh: grp: 2 (over y), col: 8 (over z, x), row: 2 (over core).
Axes of the slice: x: 2, y: 2, z: 4, core: 2. Of those that a mesh axis runs over, the one named last changes fastest.
Arguments:
- left_bounds: bfloat16 [4, 8, 128, 8, 128], P(('grp', 'row'), 'col'), parts along dimension 0, may hold values from -0.1875 to 0.1875
- right_bounds: bfloat16 [4, 8, 128, 8, 128], P(('grp', 'row'), 'col'), parts along dimension 0, may hold values from -0.1875 to 0.1875
- site_tensors: bfloat16 [4, 8, 2, 4096], P(('grp', 'row'), 'col'), parts along dimension 0, may hold values from -2 to 2
- configuration: int32 [4, 8], P(('grp', 'row'), 'col'), parts along dimension 0, may hold values from 0 to 1
- top_env: bfloat16 [16, 128, 8, 128], P(('grp', 'col')), parts along dimension 0, may hold values from -6 to 6
- bottom_env: bfloat16 [16, 128, 8, 128], P(('grp', 'col')), parts along dimension 0, may hold values from -6 to 6
- sketch: bfloat16 [1024, 128], replicated, may hold values from -0.1875 to 0.1875
Outputs:
- gradient: float32 [4, 8, 2, 4096], P(('grp', 'row'), 'col'), parts along dimension 0
- left_updated: bfloat16 [4, 8, 128, 8, 128], P(('grp', 'row'), 'col'), parts along dimension 0
- right_updated: bfloat16 [4, 8, 128, 8, 128], P(('grp', 'row'), 'col'), parts along dimension 0
The draws below stay inside these ranges and needn't reach their ends.
There are 2 independent parts, one for each index of `grp`. The reference program is written for one: setup_inputs(seed, part) draws one part's arguments, and reference() takes and returns one part's arrays. A program takes and returns all parts, laid end to end along the dimension named above; an argument that names none is the same for every part. Nothing has to cross between parts.
All inputs are finite; a program needn't handle non-finite values.
Results may differ from the reference program's by a relative error of at most 0.015.
Values may be sent and summed in bfloat16 or wider, within the bound.
A program may use at most 64 MiB of HBM per device.

```python
import math
import jax
import jax.numpy as jnp
from jax import lax

D = 8
PHYS = 2
CHI = 128
ROWS = 2
COLS = 8


def environment_field(key, noise, strength):
    row_key, col_key = jax.random.split(key, 2)
    row_part = jax.random.normal(row_key, (COLS, CHI, D, 1), jnp.float32)
    col_part = jax.random.normal(col_key, (COLS, 1, 1, CHI), jnp.float32)
    field = (noise + strength * row_part * col_part) / math.sqrt(1.0 + strength * strength)
    return jnp.clip(field, -6.0, 6.0).astype(jnp.bfloat16)


def environment_draw(key):
    noise_key, shared_key = jax.random.split(key, 2)
    noise = jax.random.normal(noise_key, (COLS, CHI, D, CHI), jnp.float32)
    strength = 1.2
    return environment_field(shared_key, noise, strength)


def draw_top_env(key, part):
    return environment_draw(jax.random.fold_in(key, 101))


def draw_bottom_env(key, part):
    return environment_draw(jax.random.fold_in(key, 202))


def set_ends(result, key, smallest, top_value):
    longest = result.shape.index(max(result.shape))
    spots = []
    for shift in (0, 1):
        where = [jax.random.randint(jax.random.fold_in(key, axis), (), 0, length) for axis, length in enumerate(result.shape)]
        where[longest] = (where[longest] + shift) % result.shape[longest]
        spots.append(tuple(where))
    return result.at[spots[0]].set(smallest).at[spots[1]].set(top_value)


def steps_of(rng, dims, shards, smallest, high):
    factor_of, own = 1.0, jax.random.fold_in(rng, 6)
    for axis_at, shards_of in shards:
        steps = jnp.exp(jax.random.uniform(jax.random.fold_in(own, axis_at), (shards_of,), jnp.float32, smallest / len(shards), high / len(shards)))
        factor_of = factor_of * jnp.repeat(steps, dims[axis_at] // shards_of).reshape([-1 if axis == axis_at else 1 for axis in range(len(dims))])
    return factor_of


def bell_draw(rng, extent, spread, limit, cuts=(), kind=jnp.bfloat16):
    drawn = spread * jax.random.normal(rng, extent, jnp.float32)
    if cuts:
        drawn = drawn * steps_of(rng, extent, cuts, -0.22, 0.18)
    return jnp.clip(drawn, -limit, limit).astype(kind)


def setup_inputs(seed: int = 0, part: int = 0) -> dict:
    key_of = jax.random.split(jax.random.key(seed), 8)
    part_keys = jax.random.split(jax.random.fold_in(key_of[7], part), 8)
    left_bounds = bell_draw(part_keys[0], (ROWS, COLS, CHI, D, CHI), (CHI * D) ** -0.5, 0.1875, ((0, 2), (1, 8)))
    right_bounds = bell_draw(part_keys[1], (ROWS, COLS, CHI, D, CHI), (CHI * D) ** -0.5, 0.1875, ((0, 2), (1, 8)))
    site_tensors = bell_draw(part_keys[2], (ROWS, COLS, PHYS, D**4), D ** -0.5, 2.0, ((0, 2), (1, 8)))
    configuration = set_ends(jax.random.randint(part_keys[3], (ROWS, COLS), 0, PHYS), jax.random.fold_in(part_keys[3], 1), 0, PHYS - 1).astype(jnp.int32)
    top_env = draw_top_env(jax.random.fold_in(jax.random.fold_in(key_of[7], part), 71), part)
    bottom_env = draw_bottom_env(jax.random.fold_in(jax.random.fold_in(key_of[7], part), 71), part)
    sketch = bell_draw(key_of[6], (CHI * D, CHI), (CHI * D) ** -0.5, 0.1875)
    return {"left_bounds": left_bounds, "right_bounds": right_bounds, "site_tensors": site_tensors, "configuration": configuration, "top_env": top_env, "bottom_env": bottom_env, "sketch": sketch}


def widen(array):
    return lax.optimization_barrier(array).astype(jnp.float32)

def orthonormal_basis(matrix):
    gram_matrix = jnp.dot(matrix.T.astype(jnp.float32), matrix.astype(jnp.float32), precision=lax.Precision.HIGHEST, preferred_element_type=jnp.float32)
    cholesky_factor = jnp.linalg.cholesky(gram_matrix)
    solved = lax.linalg.triangular_solve(cholesky_factor, matrix, left_side=False, lower=True, transpose_a=True)
    return solved.astype(jnp.bfloat16)

def project_row(frame_basis, boundary_row, oriented, sketch, closing):
    chi_size = boundary_row.shape[0]
    bond_size = boundary_row.shape[1]
    frame_tensor = widen(frame_basis).reshape(chi_size, bond_size, chi_size)
    partial_value = jnp.einsum('aup,akb->upkb', frame_tensor, widen(boundary_row)).astype(jnp.bfloat16)
    absorbed = jnp.einsum('upkb,kuod->pobd', widen(partial_value), widen(oriented)).astype(jnp.bfloat16)
    unfolded = widen(absorbed).reshape(chi_size * bond_size, chi_size * bond_size)
    if closing is None:
        closing = orthonormal_basis(jnp.dot(unfolded.T, widen(sketch)))
    unscaled = jnp.dot(unfolded, widen(closing))
    scaled = unscaled * lax.rsqrt(jnp.mean(unscaled * unscaled) + 1e-06)
    return (scaled.reshape(chi_size, bond_size, chi_size).astype(jnp.bfloat16), closing)

def pass_down(carried, western_row, core_row, eastern_row):
    partial_value = jnp.einsum('mun,mlb->unlb', widen(carried.astype(jnp.bfloat16)), widen(western_row)).astype(jnp.bfloat16)
    middle = jnp.einsum('unlb,luxd->nbxd', widen(partial_value), widen(core_row)).astype(jnp.bfloat16)
    return (partial_value, jnp.einsum('nbxd,nxc->bdc', widen(middle), widen(eastern_row)))

def pass_up(carried, western_row, core_row, eastern_row):
    lower_part = jnp.einsum('bdc,nxc->bdnx', widen(carried.astype(jnp.bfloat16)), widen(eastern_row)).astype(jnp.bfloat16)
    lower_mid = jnp.einsum('bdnx,luxd->bnlu', widen(lower_part), widen(core_row)).astype(jnp.bfloat16)
    return (lower_part, jnp.einsum('bnlu,mlb->mun', widen(lower_mid), widen(western_row)))

def reference(left_bounds, right_bounds, site_tensors, configuration, top_env, bottom_env, sketch):
    western_all = jnp.roll(left_bounds, 1, axis=1)
    eastern_all = jnp.roll(right_bounds, -1, axis=1)
    selection = jnp.arange(PHYS, dtype=jnp.int32)[None, None, :, None] == configuration[:, :, None, None]
    selected = lax.optimization_barrier(jnp.sum(jnp.where(selection, site_tensors, jnp.zeros_like(site_tensors)), axis=2))

    def column(packed):
        western, eastern, cores_flat, chooser, upper_edge, lower_edge = packed
        site_core = cores_flat.reshape(ROWS, D, D, D, D)
        mirrored = site_core.transpose(0, 3, 2, 1, 4)
        updated = []
        for boundary, oriented, upper, lower in ((western, site_core, upper_edge, lower_edge), (eastern, mirrored, upper_edge.transpose(2, 1, 0), lower_edge.transpose(2, 1, 0))):
            frame_basis = orthonormal_basis(upper.astype(jnp.float32).reshape(CHI * D, CHI))
            closing_edge = orthonormal_basis(lower.astype(jnp.float32).reshape(CHI * D, CHI))
            collected = []
            for position in range(ROWS):
                closing = closing_edge if position == ROWS - 1 else None
                new_row, frame_basis = project_row(frame_basis, boundary[position], oriented[position], sketch, closing)
                collected.append(new_row)
            updated.append(jnp.stack(collected))
        carried = upper_edge.astype(jnp.float32)
        partials = []
        for position in range(ROWS):
            partial_value, carried = pass_down(carried, western[position], site_core[position], eastern[position])
            partials.append(partial_value)
        carried = lower_edge.astype(jnp.float32)
        lowers = [None] * ROWS
        for position in reversed(range(ROWS)):
            lowers[position], carried = pass_up(carried, western[position], site_core[position], eastern[position])
        gradient_rows = jnp.stack([jnp.einsum('unlb,bdnx->luxd', widen(partials[position]), widen(lowers[position])).reshape(-1) for position in range(ROWS)])
        gradient = jnp.where(chooser, gradient_rows.reshape(ROWS, 1, D ** 4) * (D / CHI), 0.0)
        return (gradient, updated[0], updated[1])
    gradient, left_new, right_new = lax.map(column, (western_all.transpose(1, 0, 2, 3, 4), eastern_all.transpose(1, 0, 2, 3, 4), selected.transpose(1, 0, 2), selection.transpose(1, 0, 2, 3), top_env, bottom_env))
    return (gradient.transpose(1, 0, 2, 3), left_new.transpose(1, 0, 2, 3, 4), right_new.transpose(1, 0, 2, 3, 4))
```

```python
import jax
import jax.numpy as jnp
from jax import lax
from jax.experimental import pallas as pl
from jax.experimental.pallas import tpu as pltpu
from jax.sharding import PartitionSpec as P

HIGHEST = lax.Precision.HIGHEST
BLOCK = 8
BF16 = jnp.bfloat16
F32 = jnp.float32


def dot(lhs, rhs, dims, precision=None):
    return lax.dot_general(
        lhs, rhs, (dims, ((), ())), precision=precision, preferred_element_type=jnp.float32
    )


def spread_row(value, row):
    return jnp.broadcast_to(value[row : row + 1, :], value.shape)


def spread_lane(value, lane):
    return jnp.broadcast_to(value[:, lane : lane + 1], value.shape)


def thirds(value):
    high = value.astype(BF16).astype(F32)
    rest = value - high
    middle = rest.astype(BF16).astype(F32)
    return high, middle, rest - middle


def outer_update(factor, rows):
    fh, fm, fl = thirds(factor)
    rh, rm, rl = thirds(rows)
    lhs = jnp.concatenate([fh, fh, fh, fm, fm, fl], axis=0).astype(BF16)
    rhs = jnp.concatenate([rh, rm, rl, rh, rm, rh], axis=0).astype(BF16)
    return dot(lhs, rhs, ((0,), (0,)))


def inverse_factors(grams):
    size = grams[0].shape[0]
    ones = (
        lax.broadcasted_iota(jnp.int32, (size, size), 0)
        == lax.broadcasted_iota(jnp.int32, (size, size), 1)
    ).astype(F32)
    count = size // BLOCK
    sublane = lax.broadcasted_iota(jnp.int32, (BLOCK, size), 0)
    states = [
        [
            jnp.concatenate([part[i * BLOCK : (i + 1) * BLOCK] for part in (gram, ones)], axis=1)
            for i in range(count)
        ]
        for gram in grams
    ]
    found = [[] for _ in grams]
    for j in range(count):
        for q, blocks in enumerate(states):
            ahead = j + 1 < count
            rows, inverse = blocks[j][:, :size], blocks[j][:, size:]
            columns = [spread_lane(rows, j * BLOCK + c) for c in range(BLOCK)]
            if ahead:
                below, below_inverse = blocks[j + 1][:, :size], blocks[j + 1][:, size:]
                under = [spread_lane(below, j * BLOCK + c) for c in range(BLOCK)]
            pivots = jnp.ones_like(rows)
            for c in range(BLOCK):
                pivot = spread_row(columns[c], c)
                scale = pl.reciprocal(pivot, approx=True)
                pivots = jnp.where(sublane == c, pivot, pivots)
                lower = jnp.where(sublane > c, columns[c], 0.0)
                for k in range(c + 1, BLOCK):
                    entry = spread_row(columns[k], c)
                    if ahead:
                        under[k] = under[k] - (under[c] * entry) * scale
                    columns[k] = columns[k] - (lower * entry) * scale
                row, inverse_row = spread_row(rows, c), spread_row(inverse, c)
                factor = lower * scale
                rows = rows - factor * row
                inverse = inverse - factor * inverse_row
                if ahead:
                    factor = under[c] * scale
                    below = below - factor * row
                    below_inverse = below_inverse - factor * inverse_row
            scale = lax.rsqrt(pivots)
            rows = rows * scale
            inverse = inverse * scale
            found[q].append(inverse)
            if ahead:
                blocks[j + 1] = jnp.concatenate([below, below_inverse], axis=1)
            if j + 2 < count:
                update = outer_update(rows, jnp.concatenate([rows, inverse], axis=1))
                for t in range(j + 2, count):
                    blocks[t] = blocks[t] - update[t * BLOCK : (t + 1) * BLOCK]
    return [jnp.concatenate(blocks, axis=0) for blocks in found]


def loop(count, step, start=0, unroll=4):
    def several(i, carry):
        for j in range(unroll):
            carry = step(i * unroll + j, carry)
        return carry

    return lax.fori_loop(0, count // unroll, several, start)


def row_block(i, size):
    return pl.ds(pl.multiple_of(i * size, size), size)


def gram_of(source, size):
    precision = HIGHEST if source.dtype == jnp.float32 else None

    def step(i, total):
        block = source[row_block(i, size), :]
        return total + dot(block, block, ((0,), (0,)), precision)

    start = jnp.zeros((size, size), jnp.float32)
    return loop(source.shape[0] // size, step, start, 8)


def apply_transposed(source, inverse, out):
    size = inverse.shape[0]
    if source.dtype == jnp.float32:

        def step(i, carry):
            block = dot(source[row_block(i, size), :], inverse, ((1,), (1,)), HIGHEST)
            out[row_block(i, size), :] = block.astype(jnp.bfloat16)
            return carry

    else:
        high = inverse.astype(jnp.bfloat16)
        rest = inverse - high.astype(jnp.float32)
        middle = rest.astype(jnp.bfloat16)
        low = (rest - middle.astype(jnp.float32)).astype(jnp.bfloat16)

        def step(i, carry):
            block = source[row_block(i, size), :]
            total = dot(block, low, ((1,), (1,)))
            total = total + dot(block, middle, ((1,), (1,)))
            total = total + dot(block, high, ((1,), (1,)))
            out[row_block(i, size), :] = total.astype(jnp.bfloat16)
            return carry

    loop(source.shape[0] // size, step, unroll=8)


def half(value):
    return value.astype(BF16)


def flat(ref):
    outer, inner, lane = ref.shape
    return ref.reshape(outer * inner, lane)


def split_legs(matrix, rows_ref, count):
    size = rows_ref.shape[0] // count
    rows_ref[...] = matrix.astype(jnp.float32)
    return [half(rows_ref[pl.ds(leg, size, stride=count), :]) for leg in range(count)]


def stack(planes, target):
    size = planes[0].shape[0]
    for i, plane in enumerate(planes):
        target[i * size : (i + 1) * size, :] = plane


def project(planes, boundary, target):
    size = planes.shape[1]
    count = planes.shape[0] // size
    rows = flat(target)

    def step(u, carry):
        product = dot(planes[row_block(u, size), :], boundary, ((0,), (0,)))
        for k in range(count):
            rows[pl.ds(u * count + k, size, stride=count * count), :] = product[
                :, k * size : (k + 1) * size
            ]
        return carry

    loop(count, step)


def pair_up(matrix, others, swap, target):
    outer, inner, lane = target.shape
    bond = matrix.shape[0] // outer
    dims = ((1,), (1,)) if swap else ((1,), (0,))
    left = matrix[...]

    def step(d, carry):
        product = dot(left, others[row_block(d, lane), :], dims)
        target[:, row_block(d, bond), :] = product.reshape(outer, bond, lane)
        return carry

    loop(bond, step)


def mix(weights, source, store):
    outer, inner, lane = source.shape
    rows = flat(source)
    group = 8

    def step(i, carry):
        blocks = []
        for j in range(group):
            begin = pl.multiple_of((i * group + j) * inner, inner)
            blocks.append(half(rows[pl.ds(begin, inner), :]))
        product = dot(weights, jnp.concatenate(blocks, axis=1), ((1,), (0,)))
        for j in range(group):
            store(i * group + j, product[:, j * lane : (j + 1) * lane])
        return carry

    loop(outer // group, step)


def store_natural(target):
    inner = target.shape[1]
    rows = flat(target)

    def store(index, block):
        rows[pl.ds(pl.multiple_of(index * inner, inner), inner), :] = block

    return store


def store_by_leg(target, bond):
    length = target.shape[0] * bond
    rows = flat(target)

    def store(index, block):
        for d in range(bond):
            begin = pl.multiple_of(d * length + index * bond, bond)
            rows[pl.ds(begin, bond), :] = block[d * bond : (d + 1) * bond]

    return store


def leg_block(source, d, bond):
    length = source.shape[0] * bond
    return half(flat(source)[row_block(d, length), :])


def joined(planes):
    return jnp.concatenate(planes, axis=1)


def edge_kernel(
    env_ref, left_hbm, right_hbm, left_out, right_out, west_out, east_out,
    rows_ref, left_ref, right_ref, send_sem, recv_sem,
):
    me = lax.axis_index("col")
    count = lax.axis_size("col")
    after, before = lax.rem(me + 1, count), lax.rem(me + count - 1, count)
    barrier = pltpu.get_barrier_semaphore()
    for other in (after, before):
        pl.semaphore_signal(
            barrier, inc=1, device_id={"col": other}, device_id_type=pl.DeviceIdType.MESH
        )
    size = env_ref.shape[1]
    planes = split_legs(env_ref[...], rows_ref, env_ref.shape[0] // size)
    stack(planes, left_ref)
    stack([plane.T for plane in planes], right_ref)
    grams = [gram_of(left_ref, size), gram_of(right_ref, size)]
    pl.semaphore_wait(barrier, 2)
    copies = [
        pltpu.make_async_remote_copy(
            src_ref=source,
            dst_ref=target,
            send_sem=send_sem.at[i],
            recv_sem=recv_sem.at[i],
            device_id={"col": other},
            device_id_type=pl.DeviceIdType.MESH,
        )
        for i, (source, target, other) in enumerate(
            ((left_hbm, west_out, after), (right_hbm, east_out, before))
        )
    ]
    for copy in copies:
        copy.start()
    inverses = inverse_factors(grams)
    apply_transposed(left_ref, inverses[0], left_out)
    apply_transposed(right_ref, inverses[1], right_out)
    for copy in copies:
        copy.wait()


def upper_kernel(
    left_base, right_base, west_ref, east_ref, left_mix, right_mix, sketch_ref,
    next_ref, left_bulk, right_bulk, rows_ref, part_ref, absorbed_ref, left_sum, right_sum,
):
    size = west_ref.shape[1]
    bond = west_ref.shape[0] // size
    for base, boundary, weights, bulk, total in (
        (left_base, west_ref, left_mix, left_bulk, left_sum),
        (right_base, east_ref, right_mix, right_bulk, right_sum),
    ):
        project(base, joined(split_legs(boundary[...], rows_ref, bond)), part_ref)
        mix(weights[...], part_ref, store_by_leg(absorbed_ref, bond))

        def step(d, carry, bulk=bulk, total=total):
            block = leg_block(absorbed_ref, d, bond)
            bulk[d] = block
            total[row_block(d, size), :] = dot(block, sketch_ref[...], ((0,), (0,)))
            return carry

        loop(bond, step)
    inverses = inverse_factors([gram_of(left_sum, size), gram_of(right_sum, size)])
    length = left_sum.shape[0]
    apply_transposed(left_sum, inverses[0], next_ref.at[:length])
    apply_transposed(right_sum, inverses[1], next_ref.at[length:])


def lower_kernel(
    left_edge, right_edge, west_ref, east_ref, left_mix, right_mix,
    left_bulk, right_bulk, first_ref, mixed_ref,
):
    size = west_ref.shape[1]
    bond = west_ref.shape[0] // size
    steps = bond * bond
    for edge, boundary, weights, bulk in (
        (left_edge, west_ref, left_mix, left_bulk),
        (right_edge, east_ref, right_mix, right_bulk),
    ):
        pair_up(boundary, edge, False, first_ref)
        mix(weights[...], first_ref, store_natural(mixed_ref))

        def step(o, carry, bulk=bulk):
            for u in range(bond):
                bulk[o, u * size : (u + 1) * size, :] = half(
                    flat(mixed_ref)[pl.ds(u * bond + o, size, stride=steps), :]
                )
            return carry

        loop(bond, step)


def down_kernel(
    env_ref, west_ref, east_ref, weights, kept_ref, state_ref,
    rows_ref, planes_ref, first_ref, mixed_ref,
):
    size = west_ref.shape[1]
    bond = west_ref.shape[0] // size
    west = joined(split_legs(west_ref[...], rows_ref, bond))
    stack(split_legs(env_ref[...], rows_ref, bond), planes_ref)
    project(planes_ref, west, first_ref)
    mix(weights[...], first_ref, store_by_leg(mixed_ref, bond))
    kept_ref[...] = half(first_ref[...])

    def down(d, carry):
        block = leg_block(mixed_ref, d, bond)
        state_ref[row_block(d, size), :] = half(dot(block, east_ref[...], ((0,), (0,))))
        return carry

    loop(bond, down)


def up_kernel(
    env_ref, west_ref, east_ref, weights, kept_ref, state_ref,
    rows_ref, planes_ref, second_ref, mixed_ref,
):
    size = west_ref.shape[1]
    bond = west_ref.shape[0] // size
    west = joined(split_legs(west_ref[...], rows_ref, bond))
    stack(split_legs(env_ref[...], rows_ref, bond), planes_ref)
    pair_up(east_ref, planes_ref, True, second_ref)
    mix(weights[...], second_ref, store_natural(mixed_ref))
    kept_ref[...] = half(second_ref[...])

    def up(u, carry):
        low = joined(
            [
                half(flat(mixed_ref)[pl.ds(u * bond + k, size, stride=bond * bond), :])
                for k in range(bond)
            ]
        )
        state_ref[row_block(u, size), :] = half(dot(west, low, ((1,), (1,))))
        return carry

    loop(bond, up)


def upper_gradient(state_ref, east_ref, kept_ref, out_ref, volume_ref):
    pair_up(east_ref, state_ref, True, volume_ref)
    overlap(kept_ref, volume_ref, out_ref)


def lower_gradient(state_ref, west_ref, kept_ref, out_ref, rows_ref, volume_ref):
    bond = west_ref.shape[0] // west_ref.shape[1]
    project(state_ref, joined(split_legs(west_ref[...], rows_ref, bond)), volume_ref)
    overlap(volume_ref, kept_ref, out_ref)


def overlap(part_ref, key_ref, out_ref):
    outer, inner, lane = part_ref.shape
    group = 8

    def gather(ref, i):
        rows = flat(ref)
        return joined(
            [
                half(rows[pl.ds(pl.multiple_of((i * group + j) * inner, inner), inner), :])
                for j in range(group)
            ]
        )

    def step(i, total):
        return total + dot(gather(part_ref, i), gather(key_ref, i), ((1,), (1,)))

    out_ref[...] = lax.fori_loop(
        0, outer // group, step, jnp.zeros((inner, inner), jnp.float32)
    )


def upper_end_kernel(
    left_bulk, right_bulk, basis_ref, left_out, right_out, rows_ref
):
    for bulk, basis, out in (
        (left_bulk, basis_ref.at[: basis_ref.shape[0] // 2], left_out),
        (right_bulk, basis_ref.at[basis_ref.shape[0] // 2 :], right_out),
    ):
        bond, length, size = bulk.shape

        def step(i, total, bulk=bulk, basis=basis):
            rows = row_block(i, size)
            block = dot(
                joined([bulk[d, rows, :] for d in range(bond)]), basis[...], ((1,), (0,))
            )
            rows_ref[rows, :] = block
            return total + jnp.sum(block * block, axis=0, keepdims=True)

        scaled_out(loop(length // size, step, jnp.zeros((1, size)), 8), rows_ref, out)


def scaled_out(total, rows_ref, out):
    mean = jnp.sum(total, keepdims=True) * (1.0 / (rows_ref.shape[0] * rows_ref.shape[1]))
    out[...] = half(rows_ref[...] * lax.rsqrt(mean + 1e-06))


def lower_end_kernel(
    left_bulk, right_bulk, basis_ref, left_out, right_out, rows_ref
):
    for bulk, basis, out in (
        (left_bulk, basis_ref.at[: basis_ref.shape[0] // 2], left_out),
        (right_bulk, basis_ref.at[basis_ref.shape[0] // 2 :], right_out),
    ):
        bond, length, size = bulk.shape
        flipped = basis[...].T

        def step(o, total, bulk=bulk, flipped=flipped):
            block = dot(flipped, bulk[o], ((1,), (0,)))
            rows_ref[pl.ds(o, size, stride=bond), :] = block
            return total + jnp.sum(block * block, axis=0, keepdims=True)

        scaled_out(loop(bond, step, jnp.zeros((1, size)), 8), rows_ref, out)


def run(kernel, outs, scratch, flops, *args):
    in_vmem = pl.BlockSpec(memory_space=pltpu.VMEM)
    return pl.pallas_call(
        kernel,
        out_shape=tuple(jax.ShapeDtypeStruct(shape, kind) for shape, kind in outs),
        in_specs=[in_vmem] * len(args),
        out_specs=(in_vmem,) * len(outs),
        scratch_shapes=[pltpu.VMEM(shape, kind) for shape, kind in scratch],
        compiler_params=pltpu.CompilerParams(vmem_limit_bytes=48 * 1024 * 1024),
        cost_estimate=pl.CostEstimate(
            flops=flops, bytes_accessed=2_000_000, transcendentals=0
        ),
    )(*args)


def local(left_bounds, right_bounds, site_tensors, configuration, top_env, bottom_env, sketch):
    chi = left_bounds.shape[2]
    bond = left_bounds.shape[3]
    phys = site_tensors.shape[2]
    tall = (chi * bond, chi)
    wide = (bond, chi * bond, chi)
    double = (2 * chi * bond, chi)
    square = (bond * bond, bond * bond)
    volume = (chi, bond * bond, chi)
    row = lax.axis_index("row")
    leading = row == 0
    selection = (
        lax.broadcasted_iota(jnp.int32, (1, 1, phys, 1), 2) == configuration[:, :, None, None]
    )
    selected = jnp.sum(jnp.where(selection, site_tensors, jnp.zeros_like(site_tensors)), axis=2)
    core = selected.reshape(bond, bond, bond, bond)
    env = jnp.where(leading, top_env[0], bottom_env[0]).reshape(tall)
    in_vmem = pl.BlockSpec(memory_space=pltpu.VMEM)
    in_place = pl.BlockSpec(memory_space=pl.ANY)
    base_left, base_right, western, eastern = pl.pallas_call(
        edge_kernel,
        out_shape=(jax.ShapeDtypeStruct(tall, BF16),) * 4,
        in_specs=[in_vmem, in_place, in_place],
        out_specs=(in_vmem,) * 4,
        scratch_shapes=[pltpu.VMEM(tall, F32), pltpu.VMEM(tall, BF16), pltpu.VMEM(tall, BF16)]
        + [pltpu.SemaphoreType.DMA((2,))] * 2,
        compiler_params=pltpu.CompilerParams(
            vmem_limit_bytes=16 * 1024 * 1024, collective_id=0, has_side_effects=True
        ),
        cost_estimate=pl.CostEstimate(
            flops=1_000_000_000, bytes_accessed=2_000_000, transcendentals=0
        ),
    )(env, left_bounds.reshape(tall), right_bounds.reshape(tall))
    env, base_left = lax.optimization_barrier((env, base_left))
    left_mix, right_mix = (
        jnp.where(leading, core.transpose(above), core.transpose(below)).reshape(square)
        for above, below in (((3, 2, 1, 0), (1, 2, 3, 0)), ((3, 0, 1, 2), (1, 0, 3, 2)))
    )

    def first_pass(kernel, weights):
        return lambda: run(
            kernel,
            [(volume, BF16), (tall, BF16)],
            [(tall, F32), (tall, BF16), (volume, F32), (volume, F32)],
            10_000_000_000,
            env,
            western,
            eastern,
            weights,
        )

    kept, state = lax.cond(
        leading, first_pass(down_kernel, left_mix), first_pass(up_kernel, right_mix)
    )
    received = lax.ppermute(state, "row", [(0, 1), (1, 0)])

    def upper():
        return run(
            upper_kernel,
            [(double, BF16)] + [(wide, BF16)] * 2,
            [(tall, F32), (volume, F32), (volume, F32), (tall, F32), (tall, F32)],
            10_000_000_000,
            base_left,
            base_right,
            western,
            eastern,
            left_mix,
            right_mix,
            sketch,
        )

    def lower():
        bulk_left, bulk_right = run(
            lower_kernel,
            [(wide, BF16)] * 2,
            [(volume, F32)] * 2,
            10_000_000_000,
            base_left,
            base_right,
            western,
            eastern,
            left_mix,
            right_mix,
        )
        return jnp.zeros(double, BF16), bulk_left, bulk_right

    following, bulk_left, bulk_right = lax.cond(leading, upper, lower)

    def lower_part():
        (result,) = run(
            lower_gradient,
            [(square, F32)],
            [(tall, F32), (volume, F32)],
            1_000_000_000,
            received,
            western,
            kept,
        )
        return result

    grad_lower = lax.cond(leading, lambda: jnp.zeros(square, F32), lower_part)
    grad_lower, following = lax.optimization_barrier((grad_lower, following))
    sent = lax.ppermute(following, "row", [(0, 1)])

    def end(kernel, basis):
        return run(
            kernel, [(tall, BF16)] * 2, [(tall, F32)], 1_000_000_000, bulk_left, bulk_right, basis
        )

    def upper_end():
        (result,) = run(
            upper_gradient,
            [(square, F32)],
            [(volume, F32)],
            1_000_000_000,
            received,
            eastern,
            kept,
        )
        return (result, *end(upper_end_kernel, following))

    def lower_end():
        return (grad_lower, *end(lower_end_kernel, sent))

    gradient, left_new, right_new = lax.cond(leading, upper_end, lower_end)
    gradient = gradient.reshape(bond, bond, bond, bond)
    gradient = gradient.transpose(1, 0, 3, 2).reshape(1, 1, 1, bond**4)
    gradient = jnp.where(selection, gradient * (bond / chi), 0.0)
    return (
        gradient,
        left_new.reshape(left_bounds.shape),
        right_new.reshape(right_bounds.shape),
    )


def solution(mesh):
    return jax.shard_map(
        local,
        mesh=mesh,
        in_specs=(
            P(("grp", "row"), "col", None, None, None),
            P(("grp", "row"), "col", None, None, None),
            P(("grp", "row"), "col", None, None),
            P(("grp", "row"), "col"),
            P(("grp", "col"), None, None, None),
            P(("grp", "col"), None, None, None),
            P(),
        ),
        out_specs=(
            P(("grp", "row"), "col", None, None),
            P(("grp", "row"), "col", None, None, None),
            P(("grp", "row"), "col", None, None, None),
        ),
        check_vma=False,
    )
```

```python
import jax
import jax.numpy as jnp
from jax import lax
from jax.experimental import pallas as pl
from jax.experimental.pallas import tpu as pltpu
from jax.sharding import PartitionSpec as P

HIGHEST = lax.Precision.HIGHEST
BLOCK = 8
BF16 = jnp.bfloat16
F32 = jnp.float32


def dot(lhs, rhs, dims, precision=None):
    return lax.dot_general(
        lhs, rhs, (dims, ((), ())), precision=precision, preferred_element_type=jnp.float32
    )


def spread_row(value, row):
    return jnp.broadcast_to(value[row : row + 1, :], value.shape)


def spread_lane(value, lane):
    return jnp.broadcast_to(value[:, lane : lane + 1], value.shape)


def thirds(value):
    high = value.astype(BF16).astype(F32)
    rest = value - high
    middle = rest.astype(BF16).astype(F32)
    return high, middle, rest - middle


def outer_update(factor, rows):
    fh, fm, fl = thirds(factor)
    rh, rm, rl = thirds(rows)
    lhs = jnp.concatenate([fh, fh, fh, fm, fm, fl], axis=0).astype(BF16)
    rhs = jnp.concatenate([rh, rm, rl, rh, rm, rh], axis=0).astype(BF16)
    return dot(lhs, rhs, ((0,), (0,)))


def inverse_factors(grams):
    size = grams[0].shape[0]
    ones = (
        lax.broadcasted_iota(jnp.int32, (size, size), 0)
        == lax.broadcasted_iota(jnp.int32, (size, size), 1)
    ).astype(F32)
    count = size // BLOCK
    sublane = lax.broadcasted_iota(jnp.int32, (BLOCK, size), 0)
    states = [
        [
            jnp.concatenate([part[i * BLOCK : (i + 1) * BLOCK] for part in (gram, ones)], axis=1)
            for i in range(count)
        ]
        for gram in grams
    ]
    found = [[] for _ in grams]
    for j in range(count):
        for q, blocks in enumerate(states):
            ahead = j + 1 < count
            rows, inverse = blocks[j][:, :size], blocks[j][:, size:]
            columns = [spread_lane(rows, j * BLOCK + c) for c in range(BLOCK)]
            if ahead:
                below, below_inverse = blocks[j + 1][:, :size], blocks[j + 1][:, size:]
                under = [spread_lane(below, j * BLOCK + c) for c in range(BLOCK)]
            pivots = jnp.ones_like(rows)
            for c in range(BLOCK):
                pivot = spread_row(columns[c], c)
                scale = pl.reciprocal(pivot, approx=True)
                pivots = jnp.where(sublane == c, pivot, pivots)
                lower = jnp.where(sublane > c, columns[c], 0.0)
                for k in range(c + 1, BLOCK):
                    entry = spread_row(columns[k], c)
                    if ahead:
                        under[k] = under[k] - (under[c] * entry) * scale
                    columns[k] = columns[k] - (lower * entry) * scale
                row, inverse_row = spread_row(rows, c), spread_row(inverse, c)
                factor = lower * scale
                rows = rows - factor * row
                inverse = inverse - factor * inverse_row
                if ahead:
                    factor = under[c] * scale
                    below = below - factor * row
                    below_inverse = below_inverse - factor * inverse_row
            scale = lax.rsqrt(pivots)
            rows = rows * scale
            inverse = inverse * scale
            found[q].append(inverse)
            if ahead:
                blocks[j + 1] = jnp.concatenate([below, below_inverse], axis=1)
            if j + 2 < count:
                update = outer_update(rows, jnp.concatenate([rows, inverse], axis=1))
                for t in range(j + 2, count):
                    blocks[t] = blocks[t] - update[t * BLOCK : (t + 1) * BLOCK]
    return [jnp.concatenate(blocks, axis=0) for blocks in found]


def loop(count, step, start=0, unroll=4):
    def several(i, carry):
        for j in range(unroll):
            carry = step(i * unroll + j, carry)
        return carry

    return lax.fori_loop(0, count // unroll, several, start)


def rows_at(start, size):
    return pl.ds(pl.multiple_of(start, 8), size)


def half(value):
    return value.astype(BF16)


def joined(planes):
    return jnp.concatenate(planes, axis=1)


def one_hot(shape, rule):
    row = lax.broadcasted_iota(jnp.int32, shape, 0)
    column = lax.broadcasted_iota(jnp.int32, shape, 1)
    return jnp.where(rule(row, column), 1.0, 0.0)


def split_legs(matrix, rows_ref, count):
    size = rows_ref.shape[0] // count
    rows_ref[...] = matrix.astype(F32)
    return [rows_ref[pl.ds(leg, size, stride=count), :] for leg in range(count)]


def exact_parts(left, right):
    lh, lm, ll = [half(part) for part in thirds(left)]
    rh, rm, rl = [half(part) for part in thirds(right)]
    lhs = jnp.concatenate([lh, lh, lh, lm, lm, ll], axis=1)
    rhs = jnp.concatenate([rh, rm, rl, rh, rm, rh], axis=0)
    return dot(lhs, rhs, ((1,), (0,)))


def gram_of_rows(value):
    high, middle, low = [half(part) for part in thirds(value)]
    lanes = ((1,), (1,))
    cross = dot(high, middle, lanes) + dot(high, low, lanes)
    return dot(high, high, lanes) + dot(middle, middle, lanes) + (cross + cross.T)


def gram_of_columns(source, size):
    total = None
    for i in range(source.shape[0] // size):
        block = source[i * size : (i + 1) * size, :]
        block = dot(block, block, ((0,), (0,)))
        total = block if total is None else total + block
    return total


def exchange_legs(matrix, bond):
    side = bond * bond
    keep = one_hot((side, side), lambda i, j: i // bond == j // bond)
    pieces = [
        jnp.concatenate([matrix[i * bond : (i + 1) * bond]] * bond, axis=0) * keep
        for i in range(bond)
    ]
    fold = one_hot(
        (bond * side, side),
        lambda i, j: (i // side == j // bond) & (i % bond == j % bond),
    )
    return half(dot(half(joined(pieces)), half(fold), ((1,), (0,))))


def swap_order(bond):
    side = bond * bond
    return one_hot((side, side), lambda i, j: (i // bond == j % bond) & (i % bond == j // bond))


def select_core(site_ref, conf_ref, core_ref, bond):
    phys, length = site_ref.shape
    side = bond * bond
    chosen = conf_ref[...]
    total = jnp.zeros((1, length), F32)
    for p in range(phys):
        total = total + jnp.where(chosen == p, site_ref[p : p + 1, :].astype(F32), 0.0)
    count = length // (2 * side)
    pairs = jnp.concatenate(
        [total[:, i * 2 * side : (i + 1) * 2 * side] for i in range(count)], axis=0
    )
    core_ref[pl.ds(0, count, stride=2), :] = pairs
    core_ref[pl.ds(1, count, stride=2), :] = jnp.concatenate(
        [pairs[:, side:], pairs[:, :side]], axis=1
    )
    return core_ref[:, :side]


def store_gradient(value, conf_ref, core_ref, out_ref, bond, chi):
    side = bond * bond
    phys = out_ref.shape[0]
    core_ref[...] = joined([value, value])
    even = core_ref[pl.ds(0, side // 2, stride=2), :]
    odd = core_ref[pl.ds(1, side // 2, stride=2), :]
    lane = lax.broadcasted_iota(jnp.int32, even.shape, 1)
    pairs = jnp.where(lane < side, even, odd) * (bond / chi)
    line = joined([pairs[i : i + 1, :] for i in range(side // 2)])
    for p in range(phys):
        out_ref[p : p + 1, :] = jnp.where(conf_ref[...] == p, line, 0.0)


PAD = 8


def project(planes, boundary, bond, target):
    for u, plane in enumerate(planes):
        size = plane.shape[0]
        product = dot(plane, boundary, ((1,), (0,)))
        lane = boundary.shape[1] // bond
        for k in range(bond):
            target[pl.ds(k * bond + u, size, stride=bond * bond + PAD), :] = product[
                :, k * lane : (k + 1) * lane
            ]


def gathered(source, first, count, bond):
    pitch = bond * bond + PAD
    return joined(
        [
            half(source[rows_at((first + j) * pitch, bond * bond), :])
            for j in range(count)
        ]
    )


def mix_by_leg(weights, source, bond, target):
    size = target.shape[0] // (bond * bond)
    lane = target.shape[1]
    group = 8

    def step(i, carry):
        product = dot(weights, gathered(source, i * group, group, bond), ((1,), (0,)))
        for j in range(0, group, 2):
            for d in range(bond):
                block = product[d * bond : (d + 1) * bond]
                pair = [block[:, k * lane : (k + 1) * lane] for k in (j, j + 1)]
                begin = d * size * bond + (i * group + j) * bond
                target[pl.ds(pl.multiple_of(begin, 16), 2 * bond), :] = half(
                    jnp.concatenate(pair, axis=0)
                )
        return carry

    loop(size // group, step, unroll=4)


def mix_by_plane(weights, source, bond, size, target):
    lane = target.shape[1]
    group = 8

    def step(i, carry):
        product = dot(weights, gathered(source, i * group, group, bond), ((1,), (0,)))
        for j in range(group):
            target[pl.ds(i * group + j, bond * bond, stride=size + PAD), :] = product[
                :, j * lane : (j + 1) * lane
            ]
        return carry

    loop(size // group, step, unroll=4)


def plane_of(source, index, size):
    begin = index * (size + PAD)
    return half(source[begin : begin + size, :])


def pair_up(boundary, planes, bond, targets):
    lane = boundary.shape[1]
    count = boundary.shape[0] // bond
    pitch = bond * bond + PAD
    for d, plane in enumerate(planes):
        product = dot(boundary, plane, ((1,), (0,)))
        for t, target in enumerate(targets):
            block = product[:, t * lane : (t + 1) * lane]
            for a in range(count):
                begin = a * pitch + d * bond
                target[begin : begin + bond, :] = block[a * bond : (a + 1) * bond]


def overlap(left, right, bond, size):
    group = 8
    side = bond * bond

    def step(i, total):
        return total + dot(
            gathered(left, i * group, group, bond),
            gathered(right, i * group, group, bond),
            ((1,), (1,)),
        )

    return loop(size // group, step, jnp.zeros((side, side), F32), 4)


def normalised(rows_ref, target):
    value = rows_ref[...]
    mean = jnp.sum(value * value, keepdims=True) * (1.0 / value.size)
    target[...] = half(value * lax.rsqrt(mean + 1e-06))


def column_kernel(
    left_hbm, right_hbm, top_hbm, bottom_hbm, sketch_hbm, site_hbm, conf_hbm,
    grad_out, left_out, right_out,
    top_ref, bottom_ref, sketch_ref, site_ref, conf_ref, core_ref, swapped_ref, other_ref,
    bounds, extra, state_out, state_in, sent_rows,
    rows_ref, upper_ref, turned_ref, lower_ref, edge_ref,
    vol_a, vol_b, vol_c, plane_a, plane_b, legs_a, legs_b, final_ref,
    local_sem, send_sem, recv_sem,
):
    bond_rows, size = top_ref.shape
    bond = bond_rows // size
    column, row = lax.axis_index("col"), lax.axis_index("row")
    columns = lax.axis_size("col")
    after, before = lax.rem(column + 1, columns), lax.rem(column + columns - 1, columns)
    west_side, east_side = row == 0, row == 1
    mesh_id = pl.DeviceIdType.MESH

    def remote(slot, source, target, where, arrival):
        return pltpu.make_async_remote_copy(
            src_ref=source,
            dst_ref=target,
            send_sem=send_sem.at[slot],
            recv_sem=recv_sem.at[arrival],
            device_id=where,
            device_id_type=mesh_id,
        )

    barrier = pltpu.get_barrier_semaphore()
    source_column = jnp.where(west_side, before, after)
    for where in (
        {"col": source_column, "row": 0},
        {"col": source_column, "row": 1},
        {"row": 1 - row},
    ):
        pl.semaphore_signal(barrier, inc=1, device_id=where, device_id_type=mesh_id)
    locals_ = [
        pltpu.make_async_copy(source, target, local_sem.at[i])
        for i, (source, target) in enumerate(
            (
                (top_hbm, top_ref),
                (bottom_hbm, bottom_ref),
                (site_hbm, site_ref),
                (conf_hbm, conf_ref),
                (sketch_hbm, sketch_ref),
            )
        )
    ]
    for copy in locals_:
        copy.start()
    sibling = {"row": 1 - row}
    to_right = remote(0, left_hbm, bounds.at[row], {"col": after, "row": 0}, row)
    to_left = remote(1, right_hbm, bounds.at[row], {"col": before, "row": 1}, row)
    arrive = [remote(0, left_hbm, bounds.at[i], {"col": after, "row": 0}, i) for i in range(2)]
    forward = remote(2, bounds.at[1 - row], extra, sibling, 2)
    state = remote(3, state_out, state_in, sibling, 3)
    cores = remote(4, swapped_ref, other_ref, sibling, 4)
    pl.semaphore_wait(barrier, 3)

    @pl.when(west_side)
    def _():
        to_right.start()
        to_left.start()

    locals_[2].wait()
    locals_[3].wait()
    own_core = select_core(site_ref, conf_ref, core_ref, bond)
    swapped_ref[...] = exchange_legs(own_core, bond)
    own_core = half(own_core)
    cores.start()

    locals_[0].wait()
    tops = split_legs(top_ref[...], rows_ref, bond)

    @pl.when(west_side)
    def _():
        for i, plane in enumerate(tops):
            upper_ref[i * size : (i + 1) * size, :] = half(plane)
            turned_ref[i * size : (i + 1) * size, :] = half(plane.T)

    @pl.when(east_side)
    def _():
        for i, plane in enumerate(tops):
            upper_ref[i * size : (i + 1) * size, :] = half(plane.T)

    locals_[1].wait()
    bottoms = split_legs(bottom_ref[...], rows_ref, bond)

    @pl.when(west_side)
    def _():
        for i, plane in enumerate(bottoms):
            lower_ref[i * size : (i + 1) * size, :] = half(plane)

    @pl.when(east_side)
    def _():
        for i, plane in enumerate(bottoms):
            lower_ref[i * size : (i + 1) * size, :] = half(plane.T)

    grams = [gram_of_columns(upper_ref, size), gram_of_columns(lower_ref, size)]
    above, below = inverse_factors(grams)
    lanes = ((1,), (1,))
    upper, lower = upper_ref[...], lower_ref[...]
    above = [half(part) for part in thirds(above)]
    below = [half(part) for part in thirds(below)]
    basis = half(sum(dot(part, upper, lanes) for part in above[::-1]))
    edge_ref[...] = half(sum(dot(lower, part, lanes) for part in below[::-1]))

    cores.wait()
    order = half(swap_order(bond))
    first_core = jnp.where(west_side, own_core, other_ref[...])
    last_core = jnp.where(west_side, other_ref[...], own_core)
    first_mix = half(dot(order, first_core, lanes))
    last_mix = half(dot(last_core, order, lanes))
    locals_[4].wait()
    sketch = joined(
        [half(sketch_ref[i * size : (i + 1) * size, :].astype(F32).T) for i in range(bond)]
    )

    arrive[0].wait_recv()

    @pl.when(east_side)
    def _():
        forward.start()
        to_right.start()
        to_left.start()

    boundary = joined([half(part) for part in split_legs(bounds[0], rows_ref, bond)])
    project([basis[:, u * size : (u + 1) * size] for u in range(bond)], boundary, bond, vol_a)
    mix_by_leg(first_mix, vol_a, bond, legs_a)

    def contracted(rows, legs):
        parts = []
        for d in range(0, bond, 2):
            pair = [legs[(d + i) * bond * size : (d + i + 1) * bond * size, :] for i in range(2)]
            parts.append(dot(rows, joined(pair), ((1,), (0,))))
        return joined(parts)

    sums = contracted(sketch, legs_a)

    @pl.when(west_side)
    def _():
        turned = [turned_ref[u * size : (u + 1) * size, :] for u in range(bond)]
        project(turned, boundary, bond, vol_b)
        mix_by_leg(first_mix, vol_b, bond, legs_b)
        forward.wait_recv()
        east = joined(
            [half(extra[i * size : (i + 1) * size, :].astype(F32).T) for i in range(bond)]
        )
        state_out[...] = half(contracted(east, legs_b))

    (factor,) = inverse_factors([gram_of_rows(sums)])
    following = half(exact_parts(factor, sums))

    arrive[1].wait_recv()

    @pl.when(west_side)
    def _():
        forward.start()
        edges = [edge_ref[d * size : (d + 1) * size, :] for d in range(bond)]
        pair_up(bounds[1], edges, bond, [vol_a])
        mix_by_plane(last_mix, vol_a, bond, size, plane_a)

    @pl.when(east_side)
    def _():
        edges = [
            joined([ref[d * size : (d + 1) * size, :] for ref in (edge_ref, lower_ref)])
            for d in range(bond)
        ]
        pair_up(bounds[1], edges, bond, [vol_a, vol_b])
        mix_by_plane(last_mix, vol_a, bond, size, plane_a)
        mix_by_plane(last_mix, vol_b, bond, size, plane_b)
        forward.wait_recv()
        west = joined([half(part) for part in split_legs(extra[...], rows_ref, bond)])
        for u in range(bond):
            low = joined([plane_of(plane_b, l * bond + u, size) for l in range(bond)])
            state_out[:, u * size : (u + 1) * size] = half(dot(west, low, lanes))

    state.start()

    def finish_upper(target):
        block = 4 * size
        for i in range(0, bond * size, block):
            wide = joined([legs_a[d * bond * size + i : d * bond * size + i + block, :] for d in range(bond)])
            final_ref[i : i + block, :] = dot(wide, following, lanes)
        normalised(final_ref, target)

    def finish_lower(target):
        for o in range(0, bond, 2):
            pair = [
                jnp.concatenate([plane_of(plane_a, (o + i) * bond + u, size) for u in range(bond)], axis=0)
                for i in range(2)
            ]
            product = dot(following, joined(pair), ((1,), (0,)))
            for i in range(2):
                final_ref[pl.ds(o + i, size, stride=bond), :] = product[:, i * size : (i + 1) * size]
        normalised(final_ref, target)

    left_sent = remote(5, sent_rows, left_out, sibling, 5)
    right_sent = remote(5, sent_rows, right_out, sibling, 5)

    @pl.when(west_side)
    def _():
        finish_lower(sent_rows)
        left_sent.start()
        finish_upper(left_out)

    @pl.when(east_side)
    def _():
        finish_upper(sent_rows)
        right_sent.start()
        finish_lower(right_out)

    state.wait()

    def gradient_from(part, key):
        value = overlap(part, key, bond, size)
        value = dot(value, swap_order(bond), ((1,), (0,)), HIGHEST)
        store_gradient(value, conf_ref, core_ref, grad_out, bond, size)

    @pl.when(west_side)
    def _():
        planes = [state_in[:, d * size : (d + 1) * size].astype(F32).T for d in range(bond)]
        pair_up(extra[...], [half(plane) for plane in planes], bond, [vol_c])
        gradient_from(vol_b, vol_c)

    @pl.when(east_side)
    def _():
        west = joined([half(part) for part in split_legs(extra[...], rows_ref, bond)])
        project([state_in[:, u * size : (u + 1) * size] for u in range(bond)], west, bond, vol_c)
        gradient_from(vol_c, vol_b)

    to_right.wait_send()
    to_left.wait_send()
    forward.wait_send()

    @pl.when(west_side)
    def _():
        left_sent.wait()

    @pl.when(east_side)
    def _():
        right_sent.wait()


def local(left_bounds, right_bounds, site_tensors, configuration, top_env, bottom_env, sketch):
    chi = left_bounds.shape[2]
    bond = left_bounds.shape[3]
    phys = site_tensors.shape[2]
    tall = (chi * bond, chi)
    side = bond * bond
    padded = (chi * (side + PAD), chi)
    slabs = (side * (chi + PAD), chi)
    by_leg = (bond * bond * chi, chi)
    wide = (chi, bond * chi)
    in_vmem = pl.BlockSpec(memory_space=pltpu.VMEM)
    in_place = pl.BlockSpec(memory_space=pltpu.HBM)
    gradient, left_new, right_new = pl.pallas_call(
        column_kernel,
        out_shape=(
            jax.ShapeDtypeStruct((phys, bond**4), F32),
            jax.ShapeDtypeStruct(tall, BF16),
            jax.ShapeDtypeStruct(tall, BF16),
        ),
        in_specs=[in_place] * 7,
        out_specs=(in_vmem,) * 3,
        scratch_shapes=[
            pltpu.VMEM(shape, kind)
            for shape, kind in (
                (tall, BF16), (tall, BF16), (tall, BF16), ((phys, bond**4), BF16),
                ((1, 1), jnp.int32), ((side, 2 * side), F32), ((side, side), BF16),
                ((side, side), BF16), ((2, *tall), BF16), (tall, BF16), (wide, BF16),
                (wide, BF16), (tall, BF16), (tall, F32), (tall, BF16), (tall, BF16),
                (tall, BF16), (tall, BF16), (padded, F32), (padded, F32), (padded, F32),
                (slabs, F32), (slabs, F32), (by_leg, BF16), (by_leg, BF16), (tall, F32),
            )
        ]
        + [
            pltpu.SemaphoreType.DMA((5,)),
            pltpu.SemaphoreType.DMA((6,)),
            pltpu.SemaphoreType.DMA((6,)),
        ],
        compiler_params=pltpu.CompilerParams(
            vmem_limit_bytes=56 * 1024 * 1024, collective_id=0, has_side_effects=True
        ),
        cost_estimate=pl.CostEstimate(
            flops=3_000_000_000, bytes_accessed=2_000_000, transcendentals=0
        ),
    )(
        left_bounds.reshape(tall),
        right_bounds.reshape(tall),
        top_env.reshape(tall),
        bottom_env.reshape(tall),
        sketch,
        site_tensors.reshape(phys, bond**4),
        configuration,
    )
    return (
        gradient.reshape(1, 1, phys, bond**4),
        left_new.reshape(left_bounds.shape),
        right_new.reshape(right_bounds.shape),
    )


def solution(mesh):
    return jax.shard_map(
        local,
        mesh=mesh,
        in_specs=(
            P(("grp", "row"), "col", None, None, None),
            P(("grp", "row"), "col", None, None, None),
            P(("grp", "row"), "col", None, None),
            P(("grp", "row"), "col"),
            P(("grp", "col"), None, None, None),
            P(("grp", "col"), None, None, None),
            P(),
        ),
        out_specs=(
            P(("grp", "row"), "col", None, None),
            P(("grp", "row"), "col", None, None, None),
            P(("grp", "row"), "col", None, None, None),
        ),
        check_vma=False,
    )
```

```python
import functools

import jax
import jax.numpy as jnp
from jax import lax
from jax.experimental import pallas as pl
from jax.experimental.pallas import tpu as pltpu
from jax.sharding import PartitionSpec as P

HIGHEST = lax.Precision.HIGHEST
BLOCK = 8
BF16 = jnp.bfloat16
F32 = jnp.float32


def dot(lhs, rhs, dims, precision=None):
    return lax.dot_general(
        lhs, rhs, (dims, ((), ())), precision=precision, preferred_element_type=jnp.float32
    )


def spread_row(value, row):
    return jnp.broadcast_to(value[row : row + 1, :], value.shape)


def spread_lane(value, lane):
    return jnp.broadcast_to(value[:, lane : lane + 1], value.shape)


def thirds(value):
    high = value.astype(BF16).astype(F32)
    rest = value - high
    middle = rest.astype(BF16).astype(F32)
    return high, middle, rest - middle


def outer_update(factor, rows):
    fh, fm, fl = thirds(factor)
    rh, rm, rl = thirds(rows)
    lhs = jnp.concatenate([fh, fh, fh, fm, fm, fl], axis=0).astype(BF16)
    rhs = jnp.concatenate([rh, rm, rl, rh, rm, rh], axis=0).astype(BF16)
    return dot(lhs, rhs, ((0,), (0,)))


def inverse_factors(grams, beside=(), first=0):
    size = grams[0].shape[0]
    ones = (
        lax.broadcasted_iota(jnp.int32, (size, size), 0)
        == lax.broadcasted_iota(jnp.int32, (size, size), 1)
    ).astype(F32)
    count = size // BLOCK
    sublane = lax.broadcasted_iota(jnp.int32, (BLOCK, size), 0)
    states = [
        [
            jnp.concatenate([part[i * BLOCK : (i + 1) * BLOCK] for part in (gram, ones)], axis=1)
            for i in range(count)
        ]
        for gram in grams
    ]
    found = [[] for _ in grams]
    beside = list(beside)
    done = 0
    for j in range(count):
        for q, blocks in enumerate(states):
            ahead = j + 1 < count
            rows, inverse = blocks[j][:, :size], blocks[j][:, size:]
            columns = [spread_lane(rows, j * BLOCK + c) for c in range(BLOCK)]
            if ahead:
                below, below_inverse = blocks[j + 1][:, :size], blocks[j + 1][:, size:]
                under = [spread_lane(below, j * BLOCK + c) for c in range(BLOCK)]
            pivots = jnp.ones_like(rows)
            for c in range(BLOCK):
                pivot = spread_row(columns[c], c)
                scale = pl.reciprocal(pivot, approx=True)
                pivots = jnp.where(sublane == c, pivot, pivots)
                lower = jnp.where(sublane > c, columns[c], 0.0)
                for k in range(c + 1, BLOCK):
                    entry = spread_row(columns[k], c)
                    if ahead:
                        under[k] = under[k] - (under[c] * entry) * scale
                    columns[k] = columns[k] - (lower * entry) * scale
                row, inverse_row = spread_row(rows, c), spread_row(inverse, c)
                factor = lower * scale
                rows = rows - factor * row
                inverse = inverse - factor * inverse_row
                if ahead:
                    factor = under[c] * scale
                    below = below - factor * row
                    below_inverse = below_inverse - factor * inverse_row
            scale = lax.rsqrt(pivots)
            rows = rows * scale
            inverse = inverse * scale
            found[q].append(inverse)
            if ahead:
                blocks[j + 1] = jnp.concatenate([below, below_inverse], axis=1)
            if j + 2 < count:
                update = outer_update(rows, jnp.concatenate([rows, inverse], axis=1))
                for t in range(j + 2, count):
                    blocks[t] = blocks[t] - update[t * BLOCK : (t + 1) * BLOCK]
        due = len(beside) * max(j + 1 - first, 0) // (count - first)
        for step in beside[done:due]:
            step()
        done = max(done, due)
    return [jnp.concatenate(blocks, axis=0) for blocks in found]


def loop(count, step, start=0, unroll=4):
    def several(i, carry):
        for j in range(unroll):
            carry = step(i * unroll + j, carry)
        return carry

    return lax.fori_loop(0, count // unroll, several, start)


def rows_at(start, size):
    return pl.ds(pl.multiple_of(start, 8), size)


def half(value):
    return value.astype(BF16)


def joined(planes):
    return jnp.concatenate(planes, axis=1)


def one_hot(shape, rule):
    row = lax.broadcasted_iota(jnp.int32, shape, 0)
    column = lax.broadcasted_iota(jnp.int32, shape, 1)
    return jnp.where(rule(row, column), 1.0, 0.0)


def split_legs(matrix, rows_ref, count):
    size = rows_ref.shape[0] // count
    rows_ref[...] = matrix.astype(F32)
    return [rows_ref[pl.ds(leg, size, stride=count), :] for leg in range(count)]


def exact_parts(left, right):
    lh, lm, ll = [half(part) for part in thirds(left)]
    rh, rm, rl = [half(part) for part in thirds(right)]
    lhs = jnp.concatenate([lh, lh, lh, lm, lm, ll], axis=1)
    rhs = jnp.concatenate([rh, rm, rl, rh, rm, rh], axis=0)
    return dot(lhs, rhs, ((1,), (0,)))


def gram_of_rows(value):
    high, middle, low = [half(part) for part in thirds(value)]
    lanes = ((1,), (1,))
    cross = dot(high, middle, lanes) + dot(high, low, lanes)
    return dot(high, high, lanes) + dot(middle, middle, lanes) + (cross + cross.T)


def gram_of_columns(source, size):
    total = None
    for i in range(source.shape[0] // size):
        block = source[i * size : (i + 1) * size, :]
        block = dot(block, block, ((0,), (0,)))
        total = block if total is None else total + block
    return total


def exchange_legs(matrix, bond):
    side = bond * bond
    keep = one_hot((side, side), lambda i, j: i // bond == j // bond)
    pieces = [
        jnp.concatenate([matrix[i * bond : (i + 1) * bond]] * bond, axis=0) * keep
        for i in range(bond)
    ]
    fold = one_hot(
        (bond * side, side),
        lambda i, j: (i // side == j // bond) & (i % bond == j % bond),
    )
    return half(dot(half(joined(pieces)), half(fold), ((1,), (0,))))


def swap_order(bond):
    side = bond * bond
    return one_hot((side, side), lambda i, j: (i // bond == j % bond) & (i % bond == j // bond))


def select_core(site_ref, conf_ref, core_ref, bond):
    phys, length = site_ref.shape
    side = bond * bond
    chosen = conf_ref[...]
    total = jnp.zeros((1, length), F32)
    for p in range(phys):
        total = total + jnp.where(chosen == p, site_ref[p : p + 1, :].astype(F32), 0.0)
    count = length // (2 * side)
    pairs = jnp.concatenate(
        [total[:, i * 2 * side : (i + 1) * 2 * side] for i in range(count)], axis=0
    )
    core_ref[pl.ds(0, count, stride=2), :] = pairs
    core_ref[pl.ds(1, count, stride=2), :] = jnp.concatenate(
        [pairs[:, side:], pairs[:, :side]], axis=1
    )
    return core_ref[:, :side]


def store_gradient(value, conf_ref, core_ref, out_ref, bond, chi):
    side = bond * bond
    phys = out_ref.shape[0]
    core_ref[...] = joined([value, value])
    even = core_ref[pl.ds(0, side // 2, stride=2), :]
    odd = core_ref[pl.ds(1, side // 2, stride=2), :]
    lane = lax.broadcasted_iota(jnp.int32, even.shape, 1)
    pairs = jnp.where(lane < side, even, odd) * (bond / chi)
    line = joined([pairs[i : i + 1, :] for i in range(side // 2)])
    for p in range(phys):
        out_ref[p : p + 1, :] = jnp.where(conf_ref[...] == p, line, 0.0)


PAD = 8
FIRST = 5


def project_steps(planes, boundary, bond, target):
    def step(u):
        plane = planes(u)
        size = plane.shape[0]
        wide = boundary()
        product = dot(plane, wide, ((1,), (0,)))
        lane = wide.shape[1] // bond
        for k in range(bond):
            target[pl.ds(k * bond + u, size, stride=bond * bond + PAD), :] = product[
                :, k * lane : (k + 1) * lane
            ]

    return [functools.partial(step, u) for u in range(bond)]


def gathered(source, first, count, bond):
    pitch = bond * bond + PAD
    return joined(
        [
            half(source[rows_at((first + j) * pitch, bond * bond), :])
            for j in range(count)
        ]
    )


GROUP = 8


def mix_by_leg_steps(weights, source, bond, target):
    size = target.shape[0] // (bond * bond)
    lane = target.shape[1]

    def step(i):
        product = dot(weights(), gathered(source, i * GROUP, GROUP, bond), ((1,), (0,)))
        for j in range(0, GROUP, 2):
            for d in range(bond):
                block = product[d * bond : (d + 1) * bond]
                pair = [block[:, k * lane : (k + 1) * lane] for k in (j, j + 1)]
                begin = d * size * bond + (i * GROUP + j) * bond
                target[begin : begin + 2 * bond, :] = half(jnp.concatenate(pair, axis=0))

    return [functools.partial(step, i) for i in range(size // GROUP)]


def mix_by_plane_steps(weights, source, bond, size, target):
    lane = target.shape[1]

    def step(i):
        product = dot(weights(), gathered(source, i * GROUP, GROUP, bond), ((1,), (0,)))
        for j in range(GROUP):
            target[pl.ds(i * GROUP + j, bond * bond, stride=size + PAD), :] = product[
                :, j * lane : (j + 1) * lane
            ]

    return [functools.partial(step, i) for i in range(size // GROUP)]


def run_steps(steps):
    for step in steps:
        step()


def plane_of(source, index, size):
    begin = index * (size + PAD)
    return half(source[begin : begin + size, :])


def pair_up_steps(boundary, planes, bond, targets):
    pitch = bond * bond + PAD

    def step(d):
        rows = boundary()
        lane = rows.shape[1]
        count = rows.shape[0] // bond
        product = dot(rows, planes(d), ((1,), (0,)))
        for t, target in enumerate(targets):
            block = product[:, t * lane : (t + 1) * lane]
            for a in range(count):
                begin = a * pitch + d * bond
                target[begin : begin + bond, :] = block[a * bond : (a + 1) * bond]

    return [functools.partial(step, d) for d in range(bond)]


def overlap(left, right, bond, size):
    group = 8
    side = bond * bond

    def step(i, total):
        return total + dot(
            gathered(left, i * group, group, bond),
            gathered(right, i * group, group, bond),
            ((1,), (1,)),
        )

    return loop(size // group, step, jnp.zeros((side, side), F32), 4)


def normalised(rows_ref, target):
    value = rows_ref[...]
    mean = jnp.sum(value * value, keepdims=True) * (1.0 / value.size)
    target[...] = half(value * lax.rsqrt(mean + 1e-06))


def column_kernel(
    left_hbm, right_hbm, top_hbm, bottom_hbm, sketch_hbm, site_hbm, conf_hbm,
    grad_out, left_out, right_out,
    top_ref, bottom_ref, sketch_ref, site_ref, conf_ref, core_ref, swapped_ref, other_ref,
    bounds, extra, state_out, state_in, sent_rows,
    rows_ref, upper_ref, turned_ref, lower_ref, edge_ref,
    vol_a, vol_b, vol_c, plane_a, plane_b, legs_a, legs_b, final_ref,
    sketch_turned, first_mix, last_mix, basis, below_ref, first_bound, turned_bound, sums,
    following,
    local_sem, send_sem, recv_sem,
):
    bond_rows, size = top_ref.shape
    bond = bond_rows // size
    column, row = lax.axis_index("col"), lax.axis_index("row")
    columns = lax.axis_size("col")
    after, before = lax.rem(column + 1, columns), lax.rem(column + columns - 1, columns)
    west_side, east_side = row == 0, row == 1
    mesh_id = pl.DeviceIdType.MESH

    def remote(slot, source, target, where, arrival):
        return pltpu.make_async_remote_copy(
            src_ref=source,
            dst_ref=target,
            send_sem=send_sem.at[slot],
            recv_sem=recv_sem.at[arrival],
            device_id=where,
            device_id_type=mesh_id,
        )

    barrier = pltpu.get_barrier_semaphore()
    source_column = jnp.where(west_side, before, after)
    for where in (
        {"col": source_column, "row": 0},
        {"col": source_column, "row": 1},
        {"row": 1 - row},
    ):
        pl.semaphore_signal(barrier, inc=1, device_id=where, device_id_type=mesh_id)
    locals_ = [
        pltpu.make_async_copy(source, target, local_sem.at[i])
        for i, (source, target) in enumerate(
            (
                (top_hbm, top_ref),
                (bottom_hbm, bottom_ref),
                (site_hbm, site_ref),
                (conf_hbm, conf_ref),
                (sketch_hbm, sketch_ref),
            )
        )
    ]
    for copy in locals_:
        copy.start()
    sibling = {"row": 1 - row}
    to_right = remote(0, left_hbm, bounds.at[row], {"col": after, "row": 0}, row)
    to_left = remote(1, right_hbm, bounds.at[row], {"col": before, "row": 1}, row)
    arrive = [remote(0, left_hbm, bounds.at[i], {"col": after, "row": 0}, i) for i in range(2)]
    forward = remote(2, bounds.at[1 - row], extra, sibling, 2)
    state = remote(3, state_out, state_in, sibling, 3)
    cores = remote(4, swapped_ref, other_ref, sibling, 4)
    pl.semaphore_wait(barrier, 3)

    @pl.when(west_side)
    def _():
        to_right.start()
        to_left.start()

    locals_[2].wait()
    locals_[3].wait()
    own_core = select_core(site_ref, conf_ref, core_ref, bond)
    swapped_ref[...] = exchange_legs(own_core, bond)
    own_core = half(own_core)
    cores.start()

    locals_[0].wait()
    tops = split_legs(top_ref[...], rows_ref, bond)

    @pl.when(west_side)
    def _():
        for i, plane in enumerate(tops):
            upper_ref[i * size : (i + 1) * size, :] = half(plane)
            turned_ref[i * size : (i + 1) * size, :] = half(plane.T)

    @pl.when(east_side)
    def _():
        for i, plane in enumerate(tops):
            upper_ref[i * size : (i + 1) * size, :] = half(plane.T)

    locals_[1].wait()
    bottoms = split_legs(bottom_ref[...], rows_ref, bond)

    @pl.when(west_side)
    def _():
        for i, plane in enumerate(bottoms):
            lower_ref[i * size : (i + 1) * size, :] = half(plane)

    @pl.when(east_side)
    def _():
        for i, plane in enumerate(bottoms):
            lower_ref[i * size : (i + 1) * size, :] = half(plane.T)

    grams = [gram_of_columns(upper_ref, size), gram_of_columns(lower_ref, size)]
    lanes = ((1,), (1,))
    inner = ((1,), (0,))

    def send_last_row():
        @pl.when(east_side)
        def _():
            to_right.start()
            to_left.start()

    def turn_sketch(i):
        block = sketch_ref[i * size : (i + 1) * size, :].astype(F32).T
        sketch_turned[:, i * size : (i + 1) * size] = half(block)

    def weigh():
        cores.wait()
        order = half(swap_order(bond))
        first_core = jnp.where(west_side, own_core, other_ref[...])
        last_core = jnp.where(west_side, other_ref[...], own_core)
        first_mix[...] = half(dot(order, first_core, lanes))
        last_mix[...] = half(dot(last_core, order, lanes))

    locals_[4].wait()
    above, below = inverse_factors(
        grams,
        [functools.partial(turn_sketch, i) for i in range(bond)]
        + [lambda: None] * 3 + [send_last_row] + [lambda: None] * 4,
    )
    upper = upper_ref[...]
    basis[...] = half(sum(dot(half(part), upper, lanes) for part in thirds(above)[::-1]))
    for i, part in enumerate(thirds(below)):
        below_ref[i * size : (i + 1) * size, :] = half(part)
    weigh()

    def close_edge(d):
        rows = lower_ref[d * size : (d + 1) * size, :]
        parts = [below_ref[i * size : (i + 1) * size, :] for i in (2, 1, 0)]
        edge_ref[d * size : (d + 1) * size, :] = half(
            sum(dot(rows, part, lanes) for part in parts)
        )

    arrive[0].wait_recv()

    @pl.when(east_side)
    def _():
        forward.start()

    first_bound[...] = joined([half(part) for part in split_legs(bounds[0], rows_ref, bond)])
    run_steps(
        project_steps(
            lambda u: basis[:, u * size : (u + 1) * size], lambda: first_bound[...], bond, vol_a
        )
    )
    run_steps(mix_by_leg_steps(lambda: first_mix[...], vol_a, bond, legs_a))

    def contract(rows, legs, d):
        pair = [legs[(d + i) * bond * size : (d + i + 1) * bond * size, :] for i in range(2)]
        return dot(rows, joined(pair), inner)

    for d in range(0, bond, 2):
        sums[:, d * size : (d + 2) * size] = contract(sketch_turned[...], legs_a, d)
    gram = gram_of_rows(sums[...])
    edges = [functools.partial(close_edge, d) for d in range(bond)]

    def follow(factor):
        following[...] = half(exact_parts(factor, sums[...]))

    @pl.when(west_side)
    def _():
        def turn_east(i):
            block = extra[i * size : (i + 1) * size, :].astype(F32).T
            turned_bound[:, i * size : (i + 1) * size] = half(block)

        def descend(d):
            state_out[:, d * size : (d + 2) * size] = half(
                contract(turned_bound[...], legs_b, d)
            )

        def lower_row():
            arrive[1].wait_recv()
            forward.start()

        steps = (
            project_steps(
                lambda u: turned_ref[u * size : (u + 1) * size, :],
                lambda: first_bound[...],
                bond,
                vol_b,
            )
            + mix_by_leg_steps(lambda: first_mix[...], vol_b, bond, legs_b)
            + [forward.wait_recv]
            + [functools.partial(turn_east, i) for i in range(bond)]
            + [functools.partial(descend, d) for d in range(0, bond, 2)]
            + [state.start]
            + edges
            + [lower_row]
            + pair_up_steps(
                lambda: bounds[1],
                lambda d: edge_ref[d * size : (d + 1) * size, :],
                bond,
                [vol_a],
            )
            + mix_by_plane_steps(lambda: last_mix[...], vol_a, bond, size, plane_a)
        )
        (factor,) = inverse_factors([gram], steps)
        follow(factor)

    @pl.when(east_side)
    def _():
        (factor,) = inverse_factors(
            [gram],
            edges
            + [arrive[1].wait_recv]
            + pair_up_steps(
                lambda: bounds[1],
                lambda d: joined(
                    [ref[d * size : (d + 1) * size, :] for ref in (edge_ref, lower_ref)]
                ),
                bond,
                [vol_a, vol_b],
            )
            + mix_by_plane_steps(lambda: last_mix[...], vol_b, bond, size, plane_b)
            + mix_by_plane_steps(lambda: last_mix[...], vol_a, bond, size, plane_a),
            FIRST,
        )
        follow(factor)
        forward.wait_recv()
        west = joined([half(part) for part in split_legs(extra[...], rows_ref, bond)])
        turned_bound[...] = west
        for u in range(bond):
            low = joined([plane_of(plane_b, l * bond + u, size) for l in range(bond)])
            state_out[:, u * size : (u + 1) * size] = half(dot(west, low, lanes))
        state.start()


    def finish_upper(target):
        block = 4 * size
        for i in range(0, bond * size, block):
            wide = joined([legs_a[d * bond * size + i : d * bond * size + i + block, :] for d in range(bond)])
            final_ref[i : i + block, :] = dot(wide, following[...], lanes)
        normalised(final_ref, target)

    def finish_lower(target):
        for o in range(0, bond, 2):
            pair = [
                jnp.concatenate([plane_of(plane_a, (o + i) * bond + u, size) for u in range(bond)], axis=0)
                for i in range(2)
            ]
            product = dot(following[...], joined(pair), inner)
            for i in range(2):
                final_ref[pl.ds(o + i, size, stride=bond), :] = product[:, i * size : (i + 1) * size]
        normalised(final_ref, target)

    left_sent = remote(5, sent_rows, left_out, sibling, 5)
    right_sent = remote(5, sent_rows, right_out, sibling, 5)

    @pl.when(west_side)
    def _():
        finish_lower(sent_rows)
        left_sent.start()
        finish_upper(left_out)

    @pl.when(east_side)
    def _():
        finish_upper(sent_rows)
        right_sent.start()
        finish_lower(right_out)

    state.wait()

    def gradient_from(part, key):
        value = overlap(part, key, bond, size)
        value = dot(value, swap_order(bond), ((1,), (0,)), HIGHEST)
        store_gradient(value, conf_ref, core_ref, grad_out, bond, size)

    @pl.when(west_side)
    def _():
        run_steps(
            pair_up_steps(
                lambda: extra[...],
                lambda d: half(state_in[:, d * size : (d + 1) * size].astype(F32).T),
                bond,
                [vol_c],
            )
        )
        gradient_from(vol_b, vol_c)

    @pl.when(east_side)
    def _():
        run_steps(
            project_steps(
                lambda u: state_in[:, u * size : (u + 1) * size],
                lambda: turned_bound[...],
                bond,
                vol_c,
            )
        )
        gradient_from(vol_c, vol_b)

    to_right.wait_send()
    to_left.wait_send()
    forward.wait_send()

    @pl.when(west_side)
    def _():
        left_sent.wait()

    @pl.when(east_side)
    def _():
        right_sent.wait()


def emit_kernel(first, second, third, first_out, second_out, third_out, semaphores):
    pairs = ((first, first_out), (second, second_out), (third, third_out))
    copies = [
        pltpu.make_async_copy(source, target, semaphores.at[i])
        for i, (source, target) in enumerate(pairs)
    ]
    for copy in copies:
        copy.start()
    for copy in copies:
        copy.wait()


def local(left_bounds, right_bounds, site_tensors, configuration, top_env, bottom_env, sketch):
    chi = left_bounds.shape[2]
    bond = left_bounds.shape[3]
    phys = site_tensors.shape[2]
    tall = (chi * bond, chi)
    side = bond * bond
    padded = (chi * (side + PAD), chi)
    slabs = (side * (chi + PAD), chi)
    by_leg = (bond * bond * chi, chi)
    wide = (chi, bond * chi)
    in_vmem = pl.BlockSpec(memory_space=pltpu.VMEM)
    in_place = pl.BlockSpec(memory_space=pltpu.HBM)
    gradient, left_new, right_new = pl.pallas_call(
        column_kernel,
        out_shape=(
            jax.ShapeDtypeStruct((phys, bond**4), F32),
            jax.ShapeDtypeStruct(tall, BF16),
            jax.ShapeDtypeStruct(tall, BF16),
        ),
        in_specs=[in_place] * 7,
        out_specs=(in_vmem,) * 3,
        scratch_shapes=[
            pltpu.VMEM(shape, kind)
            for shape, kind in (
                (tall, BF16), (tall, BF16), (tall, BF16), ((phys, bond**4), BF16),
                ((1, 1), jnp.int32), ((side, 2 * side), F32), ((side, side), BF16),
                ((side, side), BF16), ((2, *tall), BF16), (tall, BF16), (wide, BF16),
                (wide, BF16), (tall, BF16), (tall, F32), (tall, BF16), (tall, BF16),
                (tall, BF16), (tall, BF16), (padded, F32), (padded, F32), (padded, F32),
                (slabs, F32), (slabs, F32), (by_leg, BF16), (by_leg, BF16), (tall, F32),
                (wide, BF16), ((side, side), BF16), ((side, side), BF16), (wide, BF16),
                ((3 * chi, chi), BF16), (wide, BF16), (wide, BF16), (wide, F32), (wide, BF16),
            )
        ]
        + [
            pltpu.SemaphoreType.DMA((5,)),
            pltpu.SemaphoreType.DMA((6,)),
            pltpu.SemaphoreType.DMA((6,)),
        ],
        compiler_params=pltpu.CompilerParams(
            vmem_limit_bytes=54656 * 1024, collective_id=0, has_side_effects=True
        ),
        cost_estimate=pl.CostEstimate(
            flops=3_000_000_000, bytes_accessed=2_000_000, transcendentals=0
        ),
    )(
        left_bounds.reshape(tall),
        right_bounds.reshape(tall),
        top_env.reshape(tall),
        bottom_env.reshape(tall),
        sketch,
        site_tensors.reshape(phys, bond**4),
        configuration,
    )
    shapes = [jax.ShapeDtypeStruct(value.shape, value.dtype) for value in (gradient, left_new, right_new)]
    gradient, left_new, right_new = pl.pallas_call(
        emit_kernel,
        out_shape=shapes,
        in_specs=[in_vmem] * 3,
        out_specs=[in_place] * 3,
        scratch_shapes=[pltpu.SemaphoreType.DMA((3,))],
        compiler_params=pltpu.CompilerParams(vmem_limit_bytes=1024 * 1024),
    )(gradient, left_new, right_new)
    return (
        gradient.reshape(1, 1, phys, bond**4),
        left_new.reshape(left_bounds.shape),
        right_new.reshape(right_bounds.shape),
    )


def solution(mesh):
    return jax.shard_map(
        local,
        mesh=mesh,
        in_specs=(
            P(("grp", "row"), "col", None, None, None),
            P(("grp", "row"), "col", None, None, None),
            P(("grp", "row"), "col", None, None),
            P(("grp", "row"), "col"),
            P(("grp", "col"), None, None, None),
            P(("grp", "col"), None, None, None),
            P(),
        ),
        out_specs=(
            P(("grp", "row"), "col", None, None),
            P(("grp", "row"), "col", None, None, None),
            P(("grp", "row"), "col", None, None, None),
        ),
        check_vma=False,
    )
```

```python
import functools

import jax
import jax.numpy as jnp
from jax import lax
from jax.experimental import pallas as pl
from jax.experimental.pallas import tpu as pltpu
from jax.sharding import PartitionSpec as P

HIGHEST = lax.Precision.HIGHEST
BLOCK = 8
BF16 = jnp.bfloat16
F32 = jnp.float32


def dot(lhs, rhs, dims, precision=None):
    return lax.dot_general(
        lhs, rhs, (dims, ((), ())), precision=precision, preferred_element_type=jnp.float32
    )


def spread_row(value, row):
    return jnp.broadcast_to(value[row : row + 1, :], value.shape)


def spread_lane(value, lane):
    return jnp.broadcast_to(value[:, lane : lane + 1], value.shape)


def thirds(value):
    high = value.astype(BF16).astype(F32)
    rest = value - high
    middle = rest.astype(BF16).astype(F32)
    return high, middle, rest - middle


def outer_update(factor, rows):
    fh, fm, fl = thirds(factor)
    rh, rm, rl = thirds(rows)
    lhs = jnp.concatenate([fh, fh, fh, fm, fm, fl], axis=0).astype(BF16)
    rhs = jnp.concatenate([rh, rm, rl, rh, rm, rh], axis=0).astype(BF16)
    return dot(lhs, rhs, ((0,), (0,)))


def inverse_factors(grams, beside=(), first=0):
    size = grams[0].shape[0]
    ones = (
        lax.broadcasted_iota(jnp.int32, (size, size), 0)
        == lax.broadcasted_iota(jnp.int32, (size, size), 1)
    ).astype(F32)
    count = size // BLOCK
    sublane = lax.broadcasted_iota(jnp.int32, (BLOCK, size), 0)
    states = [
        [
            jnp.concatenate([part[i * BLOCK : (i + 1) * BLOCK] for part in (gram, ones)], axis=1)
            for i in range(count)
        ]
        for gram in grams
    ]
    found = [[] for _ in grams]
    beside = list(beside)
    done = 0
    for j in range(count):
        for q, blocks in enumerate(states):
            ahead = j + 1 < count
            rows, inverse = blocks[j][:, :size], blocks[j][:, size:]
            columns = [spread_lane(rows, j * BLOCK + c) for c in range(BLOCK)]
            if ahead:
                below, below_inverse = blocks[j + 1][:, :size], blocks[j + 1][:, size:]
                under = [spread_lane(below, j * BLOCK + c) for c in range(BLOCK)]
            pivots = jnp.ones_like(rows)
            for c in range(BLOCK):
                pivot = spread_row(columns[c], c)
                scale = pl.reciprocal(pivot, approx=True)
                pivots = jnp.where(sublane == c, pivot, pivots)
                lower = jnp.where(sublane > c, columns[c], 0.0)
                for k in range(c + 1, BLOCK):
                    entry = spread_row(columns[k], c)
                    if ahead:
                        under[k] = under[k] - (under[c] * entry) * scale
                    columns[k] = columns[k] - (lower * entry) * scale
                row, inverse_row = spread_row(rows, c), spread_row(inverse, c)
                factor = lower * scale
                rows = rows - factor * row
                inverse = inverse - factor * inverse_row
                if ahead:
                    factor = under[c] * scale
                    below = below - factor * row
                    below_inverse = below_inverse - factor * inverse_row
            scale = lax.rsqrt(pivots)
            rows = rows * scale
            inverse = inverse * scale
            found[q].append(inverse)
            if ahead:
                blocks[j + 1] = jnp.concatenate([below, below_inverse], axis=1)
            if j + 2 < count:
                update = outer_update(rows, jnp.concatenate([rows, inverse], axis=1))
                for t in range(j + 2, count):
                    blocks[t] = blocks[t] - update[t * BLOCK : (t + 1) * BLOCK]
        due = len(beside) * max(j + 1 - first, 0) // (count - first)
        for step in beside[done:due]:
            step()
        done = max(done, due)
    return [jnp.concatenate(blocks, axis=0) for blocks in found]


def loop(count, step, start=0, unroll=4):
    def several(i, carry):
        for j in range(unroll):
            carry = step(i * unroll + j, carry)
        return carry

    return lax.fori_loop(0, count // unroll, several, start)


def rows_at(start, size):
    return pl.ds(pl.multiple_of(start, 8), size)


def half(value):
    return value.astype(BF16)


def joined(planes):
    return jnp.concatenate(planes, axis=1)


def one_hot(shape, rule):
    row = lax.broadcasted_iota(jnp.int32, shape, 0)
    column = lax.broadcasted_iota(jnp.int32, shape, 1)
    return jnp.where(rule(row, column), 1.0, 0.0)


def split_legs(matrix, rows_ref, count):
    size = rows_ref.shape[0] // count
    rows_ref[...] = matrix.astype(F32)
    return [rows_ref[pl.ds(leg, size, stride=count), :] for leg in range(count)]


def exact_parts(left, right):
    lh, lm, ll = [half(part) for part in thirds(left)]
    rh, rm, rl = [half(part) for part in thirds(right)]
    lhs = jnp.concatenate([lh, lh, lh, lm, lm, ll], axis=1)
    rhs = jnp.concatenate([rh, rm, rl, rh, rm, rh], axis=0)
    return dot(lhs, rhs, ((1,), (0,)))


def gram_of_rows(value):
    high, middle, low = [half(part) for part in thirds(value)]
    lanes = ((1,), (1,))
    cross = dot(high, middle, lanes) + dot(high, low, lanes)
    return dot(high, high, lanes) + dot(middle, middle, lanes) + (cross + cross.T)


def gram_of_columns(source, size):
    total = None
    for i in range(source.shape[0] // size):
        block = source[i * size : (i + 1) * size, :]
        block = dot(block, block, ((0,), (0,)))
        total = block if total is None else total + block
    return total


def exchange_legs(matrix, bond):
    side = bond * bond
    keep = one_hot((side, side), lambda i, j: i // bond == j // bond)
    pieces = [
        jnp.concatenate([matrix[i * bond : (i + 1) * bond]] * bond, axis=0) * keep
        for i in range(bond)
    ]
    fold = one_hot(
        (bond * side, side),
        lambda i, j: (i // side == j // bond) & (i % bond == j % bond),
    )
    return half(dot(half(joined(pieces)), half(fold), ((1,), (0,))))


def swap_order(bond):
    side = bond * bond
    return one_hot((side, side), lambda i, j: (i // bond == j % bond) & (i % bond == j // bond))


def select_core(site_ref, conf_ref, core_ref, bond):
    phys, length = site_ref.shape
    side = bond * bond
    chosen = conf_ref[...]
    total = jnp.zeros((1, length), F32)
    for p in range(phys):
        total = total + jnp.where(chosen == p, site_ref[p : p + 1, :].astype(F32), 0.0)
    count = length // (2 * side)
    pairs = jnp.concatenate(
        [total[:, i * 2 * side : (i + 1) * 2 * side] for i in range(count)], axis=0
    )
    core_ref[pl.ds(0, count, stride=2), :] = pairs
    core_ref[pl.ds(1, count, stride=2), :] = jnp.concatenate(
        [pairs[:, side:], pairs[:, :side]], axis=1
    )
    return core_ref[:, :side]


def store_gradient(value, conf_ref, core_ref, out_ref, bond, chi):
    side = bond * bond
    phys = out_ref.shape[0]
    core_ref[...] = joined([value, value])
    even = core_ref[pl.ds(0, side // 2, stride=2), :]
    odd = core_ref[pl.ds(1, side // 2, stride=2), :]
    lane = lax.broadcasted_iota(jnp.int32, even.shape, 1)
    pairs = jnp.where(lane < side, even, odd) * (bond / chi)
    line = joined([pairs[i : i + 1, :] for i in range(side // 2)])
    for p in range(phys):
        out_ref[p : p + 1, :] = jnp.where(conf_ref[...] == p, line, 0.0)


PAD = 8
FIRST = 7


def project_steps(planes, boundary, bond, target):
    def step(u):
        plane = planes(u)
        size = plane.shape[0]
        wide = boundary()
        product = dot(plane, wide, ((1,), (0,)))
        lane = wide.shape[1] // bond
        for k in range(bond):
            target[pl.ds(k * bond + u, size, stride=bond * bond + PAD), :] = product[
                :, k * lane : (k + 1) * lane
            ]

    return [functools.partial(step, u) for u in range(bond)]


def gathered(source, first, count, bond):
    pitch = bond * bond + PAD
    return joined(
        [
            half(source[rows_at((first + j) * pitch, bond * bond), :])
            for j in range(count)
        ]
    )


GROUP = 8


def mix_by_leg_steps(weights, source, bond, target):
    size = target.shape[0] // (bond * bond)
    lane = target.shape[1]

    def step(i):
        product = dot(weights(), gathered(source, i * GROUP, GROUP, bond), ((1,), (0,)))
        for j in range(0, GROUP, 2):
            for d in range(bond):
                block = product[d * bond : (d + 1) * bond]
                pair = [block[:, k * lane : (k + 1) * lane] for k in (j, j + 1)]
                begin = d * size * bond + (i * GROUP + j) * bond
                target[begin : begin + 2 * bond, :] = half(jnp.concatenate(pair, axis=0))

    return [functools.partial(step, i) for i in range(size // GROUP)]


def mix_by_plane_steps(weights, source, bond, size, target):
    lane = target.shape[1]

    def step(i):
        product = dot(weights(), gathered(source, i * GROUP, GROUP, bond), ((1,), (0,)))
        for j in range(GROUP):
            target[pl.ds(i * GROUP + j, bond * bond, stride=size + PAD), :] = product[
                :, j * lane : (j + 1) * lane
            ]

    return [functools.partial(step, i) for i in range(size // GROUP)]


def run_steps(steps):
    for step in steps:
        step()


def plane_of(source, index, size):
    begin = index * (size + PAD)
    return half(source[begin : begin + size, :])


def pair_up_steps(boundary, planes, bond, targets):
    pitch = bond * bond + PAD

    def step(d):
        rows = boundary()
        lane = rows.shape[1]
        count = rows.shape[0] // bond
        product = dot(rows, planes(d), ((1,), (0,)))
        for t, target in enumerate(targets):
            block = product[:, t * lane : (t + 1) * lane]
            for a in range(count):
                begin = a * pitch + d * bond
                target[begin : begin + bond, :] = block[a * bond : (a + 1) * bond]

    return [functools.partial(step, d) for d in range(bond)]


def overlap(left, right, bond, size):
    group = 8
    side = bond * bond

    def step(i, total):
        return total + dot(
            gathered(left, i * group, group, bond),
            gathered(right, i * group, group, bond),
            ((1,), (1,)),
        )

    return loop(size // group, step, jnp.zeros((side, side), F32), 4)


def normalised(rows_ref, target):
    value = rows_ref[...]
    mean = jnp.sum(value * value, keepdims=True) * (1.0 / value.size)
    target[...] = half(value * lax.rsqrt(mean + 1e-06))


def column_kernel(
    left_hbm, right_hbm, top_hbm, bottom_hbm, sketch_hbm, site_hbm, conf_hbm,
    grad_out, left_out, right_out,
    top_ref, bottom_ref, sketch_ref, site_ref, conf_ref, core_ref, swapped_ref, other_ref,
    bounds, extra, state_out, state_in, sent_rows,
    rows_ref, upper_ref, turned_ref, lower_ref, edge_ref,
    vol_a, vol_b, vol_c, plane_a, plane_b, legs_a, legs_b, final_ref,
    sketch_turned, first_mix, last_mix, basis, below_ref, first_bound, turned_bound, sums,
    following,
    local_sem, send_sem, recv_sem,
):
    bond_rows, size = top_ref.shape
    bond = bond_rows // size
    column, row = lax.axis_index("col"), lax.axis_index("row")
    columns = lax.axis_size("col")
    after, before = lax.rem(column + 1, columns), lax.rem(column + columns - 1, columns)
    west_side, east_side = row == 0, row == 1
    mesh_id = pl.DeviceIdType.MESH

    def remote(slot, source, target, where, arrival):
        return pltpu.make_async_remote_copy(
            src_ref=source,
            dst_ref=target,
            send_sem=send_sem.at[slot],
            recv_sem=recv_sem.at[arrival],
            device_id=where,
            device_id_type=mesh_id,
        )

    barrier = pltpu.get_barrier_semaphore()
    source_column = jnp.where(west_side, before, after)
    for where in (
        {"col": source_column, "row": 0},
        {"col": source_column, "row": 1},
        {"row": 1 - row},
    ):
        pl.semaphore_signal(barrier, inc=1, device_id=where, device_id_type=mesh_id)
    locals_ = [
        pltpu.make_async_copy(source, target, local_sem.at[i])
        for i, (source, target) in enumerate(
            (
                (top_hbm, top_ref),
                (bottom_hbm, bottom_ref),
                (site_hbm, site_ref),
                (conf_hbm, conf_ref),
                (sketch_hbm, sketch_ref),
            )
        )
    ]
    for copy in locals_:
        copy.start()
    sibling = {"row": 1 - row}
    to_right = remote(0, left_hbm, bounds.at[row], {"col": after, "row": 0}, row)
    to_left = remote(1, right_hbm, bounds.at[row], {"col": before, "row": 1}, row)
    arrive = [remote(0, left_hbm, bounds.at[i], {"col": after, "row": 0}, i) for i in range(2)]
    forward = remote(2, bounds.at[1 - row], extra, sibling, 2)
    state = remote(3, state_out, state_in, sibling, 3)
    cores = remote(4, swapped_ref, other_ref, sibling, 4)
    def send_first_row():
        pl.semaphore_wait(barrier, 3)

        @pl.when(west_side)
        def _():
            to_right.start()
            to_left.start()

    pl.when(column > 0)(send_first_row)

    locals_[2].wait()
    locals_[3].wait()
    own_core = select_core(site_ref, conf_ref, core_ref, bond)
    swapped_ref[...] = exchange_legs(own_core, bond)
    own_core = half(own_core)
    pl.when(column > 0)(cores.start)

    locals_[0].wait()
    tops = split_legs(top_ref[...], rows_ref, bond)

    @pl.when(west_side)
    def _():
        for i, plane in enumerate(tops):
            upper_ref[i * size : (i + 1) * size, :] = half(plane)
            turned_ref[i * size : (i + 1) * size, :] = half(plane.T)

    @pl.when(east_side)
    def _():
        for i, plane in enumerate(tops):
            upper_ref[i * size : (i + 1) * size, :] = half(plane.T)

    locals_[1].wait()
    bottoms = split_legs(bottom_ref[...], rows_ref, bond)

    @pl.when(west_side)
    def _():
        for i, plane in enumerate(bottoms):
            lower_ref[i * size : (i + 1) * size, :] = half(plane)

    @pl.when(east_side)
    def _():
        for i, plane in enumerate(bottoms):
            lower_ref[i * size : (i + 1) * size, :] = half(plane.T)

    grams = [gram_of_columns(upper_ref, size), gram_of_columns(lower_ref, size)]

    @pl.when(column == 0)
    def _():
        send_first_row()
        cores.start()

    lanes = ((1,), (1,))
    inner = ((1,), (0,))

    def send_last_row():
        @pl.when(east_side)
        def _():
            to_right.start()
            to_left.start()

    def turn_sketch(i):
        block = sketch_ref[i * size : (i + 1) * size, :].astype(F32).T
        sketch_turned[:, i * size : (i + 1) * size] = half(block)

    def weigh():
        cores.wait()
        order = half(swap_order(bond))
        first_core = jnp.where(west_side, own_core, other_ref[...])
        last_core = jnp.where(west_side, other_ref[...], own_core)
        first_mix[...] = half(dot(order, first_core, lanes))
        last_mix[...] = half(dot(last_core, order, lanes))

    locals_[4].wait()
    above, below = inverse_factors(
        grams,
        [functools.partial(turn_sketch, i) for i in range(bond)]
        + [lambda: None] * 8,
    )
    upper = upper_ref[...]
    basis[...] = half(sum(dot(half(part), upper, lanes) for part in thirds(above)[::-1]))
    for i, part in enumerate(thirds(below)):
        below_ref[i * size : (i + 1) * size, :] = half(part)
    weigh()

    def close_edge(d):
        rows = lower_ref[d * size : (d + 1) * size, :]
        parts = [below_ref[i * size : (i + 1) * size, :] for i in (2, 1, 0)]
        edge_ref[d * size : (d + 1) * size, :] = half(
            sum(dot(rows, part, lanes) for part in parts)
        )

    arrive[0].wait_recv()

    @pl.when(east_side)
    def _():
        forward.start()
        to_right.start()
        to_left.start()

    first_bound[...] = joined([half(part) for part in split_legs(bounds[0], rows_ref, bond)])
    run_steps(
        project_steps(
            lambda u: basis[:, u * size : (u + 1) * size], lambda: first_bound[...], bond, vol_a
        )
    )
    run_steps(mix_by_leg_steps(lambda: first_mix[...], vol_a, bond, legs_a))

    def contract(rows, legs, d):
        pair = [legs[(d + i) * bond * size : (d + i + 1) * bond * size, :] for i in range(2)]
        return dot(rows, joined(pair), inner)

    for d in range(0, bond, 2):
        sums[:, d * size : (d + 2) * size] = contract(sketch_turned[...], legs_a, d)
    gram = gram_of_rows(sums[...])
    edges = [functools.partial(close_edge, d) for d in range(bond)]

    def follow(factor):
        following[...] = half(exact_parts(factor, sums[...]))

    @pl.when(west_side)
    def _():
        def turn_east(i):
            block = extra[i * size : (i + 1) * size, :].astype(F32).T
            turned_bound[:, i * size : (i + 1) * size] = half(block)

        def descend(d):
            state_out[:, d * size : (d + 2) * size] = half(
                contract(turned_bound[...], legs_b, d)
            )

        def lower_row():
            arrive[1].wait_recv()
            forward.start()

        steps = (
            project_steps(
                lambda u: turned_ref[u * size : (u + 1) * size, :],
                lambda: first_bound[...],
                bond,
                vol_b,
            )
            + mix_by_leg_steps(lambda: first_mix[...], vol_b, bond, legs_b)
            + [forward.wait_recv]
            + [functools.partial(turn_east, i) for i in range(bond)]
            + [functools.partial(descend, d) for d in range(0, bond, 2)]
            + [state.start]
            + edges
            + [lower_row]
            + pair_up_steps(
                lambda: bounds[1],
                lambda d: edge_ref[d * size : (d + 1) * size, :],
                bond,
                [vol_a],
            )
            + mix_by_plane_steps(lambda: last_mix[...], vol_a, bond, size, plane_a)
        )
        (factor,) = inverse_factors([gram], steps)
        follow(factor)

    @pl.when(east_side)
    def _():
        (factor,) = inverse_factors(
            [gram],
            edges
            + [arrive[1].wait_recv]
            + pair_up_steps(
                lambda: bounds[1],
                lambda d: joined(
                    [ref[d * size : (d + 1) * size, :] for ref in (edge_ref, lower_ref)]
                ),
                bond,
                [vol_a, vol_b],
            )
            + mix_by_plane_steps(lambda: last_mix[...], vol_b, bond, size, plane_b)
            + mix_by_plane_steps(lambda: last_mix[...], vol_a, bond, size, plane_a),
            FIRST,
        )
        follow(factor)
        forward.wait_recv()
        west = joined([half(part) for part in split_legs(extra[...], rows_ref, bond)])
        turned_bound[...] = west
        for u in range(bond):
            low = joined([plane_of(plane_b, l * bond + u, size) for l in range(bond)])
            state_out[:, u * size : (u + 1) * size] = half(dot(west, low, lanes))
        state.start()


    def finish_upper(target):
        block = 4 * size
        for i in range(0, bond * size, block):
            wide = joined([legs_a[d * bond * size + i : d * bond * size + i + block, :] for d in range(bond)])
            final_ref[i : i + block, :] = dot(wide, following[...], lanes)
        normalised(final_ref, target)

    def finish_lower(target):
        for o in range(0, bond, 2):
            pair = [
                jnp.concatenate([plane_of(plane_a, (o + i) * bond + u, size) for u in range(bond)], axis=0)
                for i in range(2)
            ]
            product = dot(following[...], joined(pair), inner)
            for i in range(2):
                final_ref[pl.ds(o + i, size, stride=bond), :] = product[:, i * size : (i + 1) * size]
        normalised(final_ref, target)

    left_sent = remote(5, sent_rows, left_out, sibling, 5)
    right_sent = remote(5, sent_rows, right_out, sibling, 5)

    @pl.when(west_side)
    def _():
        finish_lower(sent_rows)
        left_sent.start()
        finish_upper(left_out)

    @pl.when(east_side)
    def _():
        finish_upper(sent_rows)
        right_sent.start()
        finish_lower(right_out)

    state.wait()

    def gradient_from(part, key):
        value = overlap(part, key, bond, size)
        value = dot(value, swap_order(bond), ((1,), (0,)), HIGHEST)
        store_gradient(value, conf_ref, core_ref, grad_out, bond, size)

    @pl.when(west_side)
    def _():
        run_steps(
            pair_up_steps(
                lambda: extra[...],
                lambda d: half(state_in[:, d * size : (d + 1) * size].astype(F32).T),
                bond,
                [vol_c],
            )
        )
        gradient_from(vol_b, vol_c)

    @pl.when(east_side)
    def _():
        run_steps(
            project_steps(
                lambda u: state_in[:, u * size : (u + 1) * size],
                lambda: turned_bound[...],
                bond,
                vol_c,
            )
        )
        gradient_from(vol_c, vol_b)

    to_right.wait_send()
    to_left.wait_send()
    forward.wait_send()

    @pl.when(west_side)
    def _():
        left_sent.wait()

    @pl.when(east_side)
    def _():
        right_sent.wait()


def emit_kernel(first, second, third, first_out, second_out, third_out, semaphores):
    pairs = ((first, first_out), (second, second_out), (third, third_out))
    copies = [
        pltpu.make_async_copy(source, target, semaphores.at[i])
        for i, (source, target) in enumerate(pairs)
    ]
    for copy in copies:
        copy.start()
    for copy in copies:
        copy.wait()


def local(left_bounds, right_bounds, site_tensors, configuration, top_env, bottom_env, sketch):
    chi = left_bounds.shape[2]
    bond = left_bounds.shape[3]
    phys = site_tensors.shape[2]
    tall = (chi * bond, chi)
    side = bond * bond
    padded = (chi * (side + PAD), chi)
    slabs = (side * (chi + PAD), chi)
    by_leg = (bond * bond * chi, chi)
    wide = (chi, bond * chi)
    in_vmem = pl.BlockSpec(memory_space=pltpu.VMEM)
    in_place = pl.BlockSpec(memory_space=pltpu.HBM)
    gradient, left_new, right_new = pl.pallas_call(
        column_kernel,
        out_shape=(
            jax.ShapeDtypeStruct((phys, bond**4), F32),
            jax.ShapeDtypeStruct(tall, BF16),
            jax.ShapeDtypeStruct(tall, BF16),
        ),
        in_specs=[in_place] * 7,
        out_specs=(in_vmem,) * 3,
        scratch_shapes=[
            pltpu.VMEM(shape, kind)
            for shape, kind in (
                (tall, BF16), (tall, BF16), (tall, BF16), ((phys, bond**4), BF16),
                ((1, 1), jnp.int32), ((side, 2 * side), F32), ((side, side), BF16),
                ((side, side), BF16), ((2, *tall), BF16), (tall, BF16), (wide, BF16),
                (wide, BF16), (tall, BF16), (tall, F32), (tall, BF16), (tall, BF16),
                (tall, BF16), (tall, BF16), (padded, F32), (padded, F32), (padded, F32),
                (slabs, F32), (slabs, F32), (by_leg, BF16), (by_leg, BF16), (tall, F32),
                (wide, BF16), ((side, side), BF16), ((side, side), BF16), (wide, BF16),
                ((3 * chi, chi), BF16), (wide, BF16), (wide, BF16), (wide, F32), (wide, BF16),
            )
        ]
        + [
            pltpu.SemaphoreType.DMA((5,)),
            pltpu.SemaphoreType.DMA((6,)),
            pltpu.SemaphoreType.DMA((6,)),
        ],
        compiler_params=pltpu.CompilerParams(
            vmem_limit_bytes=54656 * 1024, collective_id=0, has_side_effects=True
        ),
        cost_estimate=pl.CostEstimate(
            flops=3_000_000_000, bytes_accessed=2_000_000, transcendentals=0
        ),
    )(
        left_bounds.reshape(tall),
        right_bounds.reshape(tall),
        top_env.reshape(tall),
        bottom_env.reshape(tall),
        sketch,
        site_tensors.reshape(phys, bond**4),
        configuration,
    )
    shapes = [jax.ShapeDtypeStruct(value.shape, value.dtype) for value in (gradient, left_new, right_new)]
    gradient, left_new, right_new = pl.pallas_call(
        emit_kernel,
        out_shape=shapes,
        in_specs=[in_vmem] * 3,
        out_specs=[in_place] * 3,
        scratch_shapes=[pltpu.SemaphoreType.DMA((3,))],
        compiler_params=pltpu.CompilerParams(vmem_limit_bytes=1024 * 1024),
    )(gradient, left_new, right_new)
    return (
        gradient.reshape(1, 1, phys, bond**4),
        left_new.reshape(left_bounds.shape),
        right_new.reshape(right_bounds.shape),
    )


def solution(mesh):
    return jax.shard_map(
        local,
        mesh=mesh,
        in_specs=(
            P(("grp", "row"), "col", None, None, None),
            P(("grp", "row"), "col", None, None, None),
            P(("grp", "row"), "col", None, None),
            P(("grp", "row"), "col"),
            P(("grp", "col"), None, None, None),
            P(("grp", "col"), None, None, None),
            P(),
        ),
        out_specs=(
            P(("grp", "row"), "col", None, None),
            P(("grp", "row"), "col", None, None, None),
            P(("grp", "row"), "col", None, None, None),
        ),
        check_vma=False,
    )
```

```python
import functools

import jax
import jax.numpy as jnp
from jax import lax
from jax.experimental import pallas as pl
from jax.experimental.pallas import tpu as pltpu
from jax.sharding import PartitionSpec as P

HIGHEST = lax.Precision.HIGHEST
BLOCK = 8
BF16 = jnp.bfloat16
F32 = jnp.float32


def dot(lhs, rhs, dims, precision=None):
    return lax.dot_general(
        lhs, rhs, (dims, ((), ())), precision=precision, preferred_element_type=jnp.float32
    )


def spread_row(value, row):
    return jnp.broadcast_to(value[row : row + 1, :], value.shape)


def spread_lane(value, lane):
    return jnp.broadcast_to(value[:, lane : lane + 1], value.shape)


def thirds(value):
    high = value.astype(BF16).astype(F32)
    rest = value - high
    middle = rest.astype(BF16).astype(F32)
    return high, middle, rest - middle


def outer_update(factor, rows):
    fh, fm, fl = thirds(factor)
    rh, rm, rl = thirds(rows)
    lhs = jnp.concatenate([fh, fh, fh, fm, fm, fl], axis=0).astype(BF16)
    rhs = jnp.concatenate([rh, rm, rl, rh, rm, rh], axis=0).astype(BF16)
    return dot(lhs, rhs, ((0,), (0,)))


def inverse_factors(grams, beside=(), first=0):
    size = grams[0].shape[0]
    ones = (
        lax.broadcasted_iota(jnp.int32, (size, size), 0)
        == lax.broadcasted_iota(jnp.int32, (size, size), 1)
    ).astype(F32)
    count = size // BLOCK
    sublane = lax.broadcasted_iota(jnp.int32, (BLOCK, size), 0)
    states = [
        [
            jnp.concatenate([part[i * BLOCK : (i + 1) * BLOCK] for part in (gram, ones)], axis=1)
            for i in range(count)
        ]
        for gram in grams
    ]
    found = [[] for _ in grams]
    beside = list(beside)
    done = 0
    for j in range(count):
        for q, blocks in enumerate(states):
            ahead = j + 1 < count
            rows, inverse = blocks[j][:, :size], blocks[j][:, size:]
            columns = [spread_lane(rows, j * BLOCK + c) for c in range(BLOCK)]
            if ahead:
                below, below_inverse = blocks[j + 1][:, :size], blocks[j + 1][:, size:]
                under = [spread_lane(below, j * BLOCK + c) for c in range(BLOCK)]
            pivots = jnp.ones_like(rows)
            for c in range(BLOCK):
                pivot = spread_row(columns[c], c)
                scale = pl.reciprocal(pivot, approx=True)
                pivots = jnp.where(sublane == c, pivot, pivots)
                lower = jnp.where(sublane > c, columns[c], 0.0)
                for k in range(c + 1, BLOCK):
                    entry = spread_row(columns[k], c)
                    if ahead:
                        under[k] = under[k] - (under[c] * entry) * scale
                    columns[k] = columns[k] - (lower * entry) * scale
                row, inverse_row = spread_row(rows, c), spread_row(inverse, c)
                factor = lower * scale
                rows = rows - factor * row
                inverse = inverse - factor * inverse_row
                if ahead:
                    factor = under[c] * scale
                    below = below - factor * row
                    below_inverse = below_inverse - factor * inverse_row
            scale = lax.rsqrt(pivots)
            rows = rows * scale
            inverse = inverse * scale
            found[q].append(inverse)
            if ahead:
                blocks[j + 1] = jnp.concatenate([below, below_inverse], axis=1)
            if j + 2 < count:
                update = outer_update(rows, jnp.concatenate([rows, inverse], axis=1))
                for t in range(j + 2, count):
                    blocks[t] = blocks[t] - update[t * BLOCK : (t + 1) * BLOCK]
        due = len(beside) * max(j + 1 - first, 0) // (count - first)
        for step in beside[done:due]:
            step()
        done = max(done, due)
    return [jnp.concatenate(blocks, axis=0) for blocks in found]


def loop(count, step, start=0, unroll=4):
    def several(i, carry):
        for j in range(unroll):
            carry = step(i * unroll + j, carry)
        return carry

    return lax.fori_loop(0, count // unroll, several, start)


def rows_at(start, size):
    return pl.ds(pl.multiple_of(start, 8), size)


def half(value):
    return value.astype(BF16)


def joined(planes):
    return jnp.concatenate(planes, axis=1)


def one_hot(shape, rule):
    row = lax.broadcasted_iota(jnp.int32, shape, 0)
    column = lax.broadcasted_iota(jnp.int32, shape, 1)
    return jnp.where(rule(row, column), 1.0, 0.0)


def split_legs(matrix, rows_ref, count):
    size = rows_ref.shape[0] // count
    rows_ref[...] = matrix.astype(F32)
    return [rows_ref[pl.ds(leg, size, stride=count), :] for leg in range(count)]


def exact_parts(left, right):
    lh, lm, ll = [half(part) for part in thirds(left)]
    rh, rm, rl = [half(part) for part in thirds(right)]
    lhs = jnp.concatenate([lh, lh, lh, lm, lm, ll], axis=1)
    rhs = jnp.concatenate([rh, rm, rl, rh, rm, rh], axis=0)
    return dot(lhs, rhs, ((1,), (0,)))


def gram_of_rows(value):
    high, middle, low = [half(part) for part in thirds(value)]
    lanes = ((1,), (1,))
    cross = dot(high, middle, lanes) + dot(high, low, lanes)
    return dot(high, high, lanes) + dot(middle, middle, lanes) + (cross + cross.T)


def gram_of_columns(source, size):
    total = None
    for i in range(source.shape[0] // size):
        block = source[i * size : (i + 1) * size, :]
        block = dot(block, block, ((0,), (0,)))
        total = block if total is None else total + block
    return total


def exchange_legs(matrix, bond):
    side = bond * bond
    keep = one_hot((side, side), lambda i, j: i // bond == j // bond)
    pieces = [
        jnp.concatenate([matrix[i * bond : (i + 1) * bond]] * bond, axis=0) * keep
        for i in range(bond)
    ]
    fold = one_hot(
        (bond * side, side),
        lambda i, j: (i // side == j // bond) & (i % bond == j % bond),
    )
    return half(dot(half(joined(pieces)), half(fold), ((1,), (0,))))


def swap_order(bond):
    side = bond * bond
    return one_hot((side, side), lambda i, j: (i // bond == j % bond) & (i % bond == j // bond))


def select_core(site_ref, conf_ref, core_ref, bond):
    phys, length = site_ref.shape
    side = bond * bond
    chosen = conf_ref[...]
    total = jnp.zeros((1, length), F32)
    for p in range(phys):
        total = total + jnp.where(chosen == p, site_ref[p : p + 1, :].astype(F32), 0.0)
    count = length // (2 * side)
    pairs = jnp.concatenate(
        [total[:, i * 2 * side : (i + 1) * 2 * side] for i in range(count)], axis=0
    )
    core_ref[pl.ds(0, count, stride=2), :] = pairs
    core_ref[pl.ds(1, count, stride=2), :] = jnp.concatenate(
        [pairs[:, side:], pairs[:, :side]], axis=1
    )
    return core_ref[:, :side]


def store_gradient(value, conf_ref, core_ref, out_ref, bond, chi):
    side = bond * bond
    phys = out_ref.shape[0]
    core_ref[...] = joined([value, value])
    even = core_ref[pl.ds(0, side // 2, stride=2), :]
    odd = core_ref[pl.ds(1, side // 2, stride=2), :]
    lane = lax.broadcasted_iota(jnp.int32, even.shape, 1)
    pairs = jnp.where(lane < side, even, odd) * (bond / chi)
    line = joined([pairs[i : i + 1, :] for i in range(side // 2)])
    for p in range(phys):
        out_ref[p : p + 1, :] = jnp.where(conf_ref[...] == p, line, 0.0)


PAD = 8
FIRST = 7


def project_steps(planes, boundary, bond, target):
    def step(u):
        plane = planes(u)
        size = plane.shape[0]
        wide = boundary()
        product = dot(plane, wide, ((1,), (0,)))
        lane = wide.shape[1] // bond
        for k in range(bond):
            target[pl.ds(k * bond + u, size, stride=bond * bond + PAD), :] = product[
                :, k * lane : (k + 1) * lane
            ]

    return [functools.partial(step, u) for u in range(bond)]


def gathered(source, first, count, bond):
    pitch = bond * bond + PAD
    return joined(
        [
            half(source[rows_at((first + j) * pitch, bond * bond), :])
            for j in range(count)
        ]
    )


GROUP = 8


def mix_by_leg_steps(weights, source, bond, target, kept=None):
    size = target.shape[0] // (bond * bond)
    lane = target.shape[1]

    def step(i):
        block = gathered(source, i * GROUP, GROUP, bond)
        if kept is not None:
            kept[i * bond * bond : (i + 1) * bond * bond, :] = block
        product = dot(weights(), block, ((1,), (0,)))
        for j in range(0, GROUP, 2):
            for d in range(bond):
                block = product[d * bond : (d + 1) * bond]
                pair = [block[:, k * lane : (k + 1) * lane] for k in (j, j + 1)]
                begin = d * size * bond + (i * GROUP + j) * bond
                target[begin : begin + 2 * bond, :] = half(jnp.concatenate(pair, axis=0))

    return [functools.partial(step, i) for i in range(size // GROUP)]


def mix_by_plane_steps(weights, source, bond, size, target, kept=None):
    lane = target.shape[1]

    def step(i):
        block = gathered(source, i * GROUP, GROUP, bond)
        if kept is not None:
            kept[i * bond * bond : (i + 1) * bond * bond, :] = block
        product = dot(weights(), block, ((1,), (0,)))
        for j in range(GROUP):
            target[pl.ds(i * GROUP + j, bond * bond, stride=size + PAD), :] = product[
                :, j * lane : (j + 1) * lane
            ]

    return [functools.partial(step, i) for i in range(size // GROUP)]


def run_steps(steps):
    for step in steps:
        step()


def plane_of(source, index, size):
    begin = index * (size + PAD)
    return half(source[begin : begin + size, :])


def pair_up_steps(boundary, planes, bond, targets):
    pitch = bond * bond + PAD

    def step(d):
        rows = boundary()
        lane = rows.shape[1]
        count = rows.shape[0] // bond
        product = dot(rows, planes(d), ((1,), (0,)))
        for t, target in enumerate(targets):
            block = product[:, t * lane : (t + 1) * lane]
            for a in range(count):
                begin = a * pitch + d * bond
                target[begin : begin + bond, :] = block[a * bond : (a + 1) * bond]

    return [functools.partial(step, d) for d in range(bond)]


def overlap(left, right, bond, size):
    side = bond * bond

    def step(i, total):
        return total + dot(left(i), right(i), ((1,), (1,)))

    return loop(size // GROUP, step, jnp.zeros((side, side), F32), 4)


def normalised(rows_ref, target):
    value = rows_ref[...]
    mean = jnp.sum(value * value, keepdims=True) * (1.0 / value.size)
    target[...] = half(value * lax.rsqrt(mean + 1e-06))


def column_kernel(
    left_hbm, right_hbm, top_hbm, bottom_hbm, sketch_hbm, site_hbm, conf_hbm,
    grad_out, left_out, right_out,
    top_ref, bottom_ref, sketch_ref, site_ref, conf_ref, core_ref, swapped_ref, other_ref,
    bounds, extra, state_out, state_in, sent_rows,
    rows_ref, upper_ref, turned_ref, lower_ref, edge_ref,
    vol_a, vol_b, vol_c, plane_a, plane_b, legs_a, legs_b, final_ref,
    sketch_turned, first_mix, last_mix, basis, below_ref, first_bound, turned_bound, sums,
    following, kept,
    local_sem, send_sem, recv_sem,
):
    bond_rows, size = top_ref.shape
    bond = bond_rows // size
    column, row = lax.axis_index("col"), lax.axis_index("row")
    columns = lax.axis_size("col")
    after, before = lax.rem(column + 1, columns), lax.rem(column + columns - 1, columns)
    west_side, east_side = row == 0, row == 1
    mesh_id = pl.DeviceIdType.MESH

    def remote(slot, source, target, where, arrival):
        return pltpu.make_async_remote_copy(
            src_ref=source,
            dst_ref=target,
            send_sem=send_sem.at[slot],
            recv_sem=recv_sem.at[arrival],
            device_id=where,
            device_id_type=mesh_id,
        )

    barrier = pltpu.get_barrier_semaphore()
    source_column = jnp.where(west_side, before, after)
    for where in (
        {"col": source_column, "row": 0},
        {"col": source_column, "row": 1},
        {"row": 1 - row},
    ):
        pl.semaphore_signal(barrier, inc=1, device_id=where, device_id_type=mesh_id)
    locals_ = [
        pltpu.make_async_copy(source, target, local_sem.at[i])
        for i, (source, target) in enumerate(
            (
                (top_hbm, top_ref),
                (bottom_hbm, bottom_ref),
                (site_hbm, site_ref),
                (conf_hbm, conf_ref),
                (sketch_hbm, sketch_ref),
            )
        )
    ]
    for copy in locals_:
        copy.start()
    sibling = {"row": 1 - row}
    to_right = remote(0, left_hbm, bounds.at[row], {"col": after, "row": 0}, row)
    to_left = remote(1, right_hbm, bounds.at[row], {"col": before, "row": 1}, row)
    arrive = [remote(0, left_hbm, bounds.at[i], {"col": after, "row": 0}, i) for i in range(2)]
    forward = remote(2, bounds.at[1 - row], extra, sibling, 2)
    state = remote(3, state_out, state_in, sibling, 3)
    cores = remote(4, swapped_ref, other_ref, sibling, 4)
    def send_first_row():
        pl.semaphore_wait(barrier, 3)

        @pl.when(west_side)
        def _():
            to_right.start()
            to_left.start()

    pl.when(column > 0)(send_first_row)

    locals_[2].wait()
    locals_[3].wait()
    own_core = select_core(site_ref, conf_ref, core_ref, bond)
    swapped_ref[...] = exchange_legs(own_core, bond)
    own_core = half(own_core)
    pl.when(column > 0)(cores.start)

    locals_[0].wait()
    tops = split_legs(top_ref[...], rows_ref, bond)

    @pl.when(west_side)
    def _():
        for i, plane in enumerate(tops):
            upper_ref[i * size : (i + 1) * size, :] = half(plane)
            turned_ref[i * size : (i + 1) * size, :] = half(plane.T)

    @pl.when(east_side)
    def _():
        for i, plane in enumerate(tops):
            upper_ref[i * size : (i + 1) * size, :] = half(plane.T)

    locals_[1].wait()
    bottoms = split_legs(bottom_ref[...], rows_ref, bond)

    @pl.when(west_side)
    def _():
        for i, plane in enumerate(bottoms):
            lower_ref[i * size : (i + 1) * size, :] = half(plane)

    @pl.when(east_side)
    def _():
        for i, plane in enumerate(bottoms):
            lower_ref[i * size : (i + 1) * size, :] = half(plane.T)

    grams = [gram_of_columns(upper_ref, size), gram_of_columns(lower_ref, size)]

    @pl.when(column == 0)
    def _():
        send_first_row()
        cores.start()

    lanes = ((1,), (1,))
    inner = ((1,), (0,))

    def send_last_row():
        @pl.when(east_side)
        def _():
            to_right.start()
            to_left.start()

    def turn_sketch(i):
        block = sketch_ref[i * size : (i + 1) * size, :].astype(F32).T
        sketch_turned[:, i * size : (i + 1) * size] = half(block)

    def weigh():
        cores.wait()
        order = half(swap_order(bond))
        first_core = jnp.where(west_side, own_core, other_ref[...])
        last_core = jnp.where(west_side, other_ref[...], own_core)
        first_mix[...] = half(dot(order, first_core, lanes))
        last_mix[...] = half(dot(last_core, order, lanes))

    locals_[4].wait()
    above, below = inverse_factors(
        grams,
        [functools.partial(turn_sketch, i) for i in range(bond)]
        + [lambda: None] * 8,
    )
    upper = upper_ref[...]
    basis[...] = half(sum(dot(half(part), upper, lanes) for part in thirds(above)[::-1]))
    for i, part in enumerate(thirds(below)):
        below_ref[i * size : (i + 1) * size, :] = half(part)
    weigh()

    def close_edge(d):
        rows = lower_ref[d * size : (d + 1) * size, :]
        parts = [below_ref[i * size : (i + 1) * size, :] for i in (2, 1, 0)]
        edge_ref[d * size : (d + 1) * size, :] = half(
            sum(dot(rows, part, lanes) for part in parts)
        )

    arrive[0].wait_recv()

    @pl.when(east_side)
    def _():
        forward.start()
        to_right.start()
        to_left.start()

    first_bound[...] = joined([half(part) for part in split_legs(bounds[0], rows_ref, bond)])
    run_steps(
        project_steps(
            lambda u: basis[:, u * size : (u + 1) * size], lambda: first_bound[...], bond, vol_a
        )
    )
    run_steps(mix_by_leg_steps(lambda: first_mix[...], vol_a, bond, legs_a))

    def contract(rows, legs, d):
        pair = [legs[(d + i) * bond * size : (d + i + 1) * bond * size, :] for i in range(2)]
        return dot(rows, joined(pair), inner)

    for d in range(0, bond, 2):
        sums[:, d * size : (d + 2) * size] = contract(sketch_turned[...], legs_a, d)
    gram = gram_of_rows(sums[...])
    edges = [functools.partial(close_edge, d) for d in range(bond)]

    def follow(factor):
        following[...] = half(exact_parts(factor, sums[...]))

    @pl.when(west_side)
    def _():
        def turn_east(i):
            block = extra[i * size : (i + 1) * size, :].astype(F32).T
            turned_bound[:, i * size : (i + 1) * size] = half(block)

        def descend(d):
            state_out[:, d * size : (d + 2) * size] = half(
                contract(turned_bound[...], legs_b, d)
            )

        def lower_row():
            arrive[1].wait_recv()
            forward.start()

        steps = (
            project_steps(
                lambda u: turned_ref[u * size : (u + 1) * size, :],
                lambda: first_bound[...],
                bond,
                vol_b,
            )
            + mix_by_leg_steps(lambda: first_mix[...], vol_b, bond, legs_b, kept)
            + [forward.wait_recv]
            + [functools.partial(turn_east, i) for i in range(bond)]
            + [functools.partial(descend, d) for d in range(0, bond, 2)]
            + [state.start]
            + edges
            + [lower_row]
            + pair_up_steps(
                lambda: bounds[1],
                lambda d: edge_ref[d * size : (d + 1) * size, :],
                bond,
                [vol_a],
            )
            + mix_by_plane_steps(lambda: last_mix[...], vol_a, bond, size, plane_a)
        )
        (factor,) = inverse_factors([gram], steps)
        follow(factor)

    @pl.when(east_side)
    def _():
        def spread_west():
            forward.wait_recv()
            turned_bound[...] = joined(
                [half(part) for part in split_legs(extra[...], rows_ref, bond)]
            )

        def ascend(u):
            low = joined([plane_of(plane_b, l * bond + u, size) for l in range(bond)])
            state_out[:, u * size : (u + 1) * size] = half(dot(turned_bound[...], low, lanes))

        (factor,) = inverse_factors(
            [gram],
            edges
            + [arrive[1].wait_recv]
            + pair_up_steps(
                lambda: bounds[1],
                lambda d: joined(
                    [ref[d * size : (d + 1) * size, :] for ref in (edge_ref, lower_ref)]
                ),
                bond,
                [vol_a, vol_b],
            )
            + mix_by_plane_steps(lambda: last_mix[...], vol_b, bond, size, plane_b, kept)
            + [spread_west]
            + [functools.partial(ascend, u) for u in range(bond)]
            + [state.start]
            + mix_by_plane_steps(lambda: last_mix[...], vol_a, bond, size, plane_a),
            FIRST,
        )
        follow(factor)

    def finish_upper(target):
        block = 4 * size
        for i in range(0, bond * size, block):
            wide = joined([legs_a[d * bond * size + i : d * bond * size + i + block, :] for d in range(bond)])
            final_ref[i : i + block, :] = dot(wide, following[...], lanes)
        normalised(final_ref, target)

    def finish_lower(target):
        for o in range(0, bond, 2):
            pair = [
                jnp.concatenate([plane_of(plane_a, (o + i) * bond + u, size) for u in range(bond)], axis=0)
                for i in range(2)
            ]
            product = dot(following[...], joined(pair), inner)
            for i in range(2):
                final_ref[pl.ds(o + i, size, stride=bond), :] = product[:, i * size : (i + 1) * size]
        normalised(final_ref, target)

    left_sent = remote(5, sent_rows, left_out, sibling, 5)
    right_sent = remote(5, sent_rows, right_out, sibling, 5)

    @pl.when(west_side)
    def _():
        finish_lower(sent_rows)
        left_sent.start()
        finish_upper(left_out)

    @pl.when(east_side)
    def _():
        finish_upper(sent_rows)
        right_sent.start()
        finish_lower(right_out)

    state.wait()

    def kept_block(i):
        side = bond * bond
        return kept[pl.ds(pl.multiple_of(i * side, side), side), :]

    def new_block(i):
        return gathered(vol_c, i * GROUP, GROUP, bond)

    def gradient_from(part, key):
        value = overlap(part, key, bond, size)
        value = dot(value, swap_order(bond), ((1,), (0,)), HIGHEST)
        store_gradient(value, conf_ref, core_ref, grad_out, bond, size)

    @pl.when(west_side)
    def _():
        run_steps(
            pair_up_steps(
                lambda: extra[...],
                lambda d: half(state_in[:, d * size : (d + 1) * size].astype(F32).T),
                bond,
                [vol_c],
            )
        )
        gradient_from(kept_block, new_block)

    @pl.when(east_side)
    def _():
        run_steps(
            project_steps(
                lambda u: state_in[:, u * size : (u + 1) * size],
                lambda: turned_bound[...],
                bond,
                vol_c,
            )
        )
        gradient_from(new_block, kept_block)

    to_right.wait_send()
    to_left.wait_send()
    forward.wait_send()

    @pl.when(west_side)
    def _():
        left_sent.wait()

    @pl.when(east_side)
    def _():
        right_sent.wait()


def emit_kernel(first, second, third, first_out, second_out, third_out, semaphores):
    pairs = ((first, first_out), (second, second_out), (third, third_out))
    copies = [
        pltpu.make_async_copy(source, target, semaphores.at[i])
        for i, (source, target) in enumerate(pairs)
    ]
    for copy in copies:
        copy.start()
    for copy in copies:
        copy.wait()


def local(left_bounds, right_bounds, site_tensors, configuration, top_env, bottom_env, sketch):
    chi = left_bounds.shape[2]
    bond = left_bounds.shape[3]
    phys = site_tensors.shape[2]
    tall = (chi * bond, chi)
    side = bond * bond
    padded = (chi * (side + PAD), chi)
    slabs = (side * (chi + PAD), chi)
    by_leg = (bond * bond * chi, chi)
    wide = (chi, bond * chi)
    in_vmem = pl.BlockSpec(memory_space=pltpu.VMEM)
    in_place = pl.BlockSpec(memory_space=pltpu.HBM)
    gradient, left_new, right_new = pl.pallas_call(
        column_kernel,
        out_shape=(
            jax.ShapeDtypeStruct((phys, bond**4), F32),
            jax.ShapeDtypeStruct(tall, BF16),
            jax.ShapeDtypeStruct(tall, BF16),
        ),
        in_specs=[in_place] * 7,
        out_specs=(in_vmem,) * 3,
        scratch_shapes=[
            pltpu.VMEM(shape, kind)
            for shape, kind in (
                (tall, BF16), (tall, BF16), (tall, BF16), ((phys, bond**4), BF16),
                ((1, 1), jnp.int32), ((side, 2 * side), F32), ((side, side), BF16),
                ((side, side), BF16), ((2, *tall), BF16), (tall, BF16), (wide, BF16),
                (wide, BF16), (tall, BF16), (tall, F32), (tall, BF16), (tall, BF16),
                (tall, BF16), (tall, BF16), (padded, F32), (padded, F32), (padded, F32),
                (slabs, F32), (slabs, F32), (by_leg, BF16), (by_leg, BF16), (tall, F32),
                (wide, BF16), ((side, side), BF16), ((side, side), BF16), (wide, BF16),
                ((3 * chi, chi), BF16), (wide, BF16), (wide, BF16), (wide, F32), (wide, BF16),
                ((side * (chi // GROUP), GROUP * chi), BF16),
            )
        ]
        + [
            pltpu.SemaphoreType.DMA((5,)),
            pltpu.SemaphoreType.DMA((6,)),
            pltpu.SemaphoreType.DMA((6,)),
        ],
        compiler_params=pltpu.CompilerParams(
            vmem_limit_bytes=54656 * 1024, collective_id=0, has_side_effects=True
        ),
        cost_estimate=pl.CostEstimate(
            flops=3_000_000_000, bytes_accessed=2_000_000, transcendentals=0
        ),
    )(
        left_bounds.reshape(tall),
        right_bounds.reshape(tall),
        top_env.reshape(tall),
        bottom_env.reshape(tall),
        sketch,
        site_tensors.reshape(phys, bond**4),
        configuration,
    )
    shapes = [jax.ShapeDtypeStruct(value.shape, value.dtype) for value in (gradient, left_new, right_new)]
    gradient, left_new, right_new = pl.pallas_call(
        emit_kernel,
        out_shape=shapes,
        in_specs=[in_vmem] * 3,
        out_specs=[in_place] * 3,
        scratch_shapes=[pltpu.SemaphoreType.DMA((3,))],
        compiler_params=pltpu.CompilerParams(vmem_limit_bytes=1024 * 1024),
    )(gradient, left_new, right_new)
    return (
        gradient.reshape(1, 1, phys, bond**4),
        left_new.reshape(left_bounds.shape),
        right_new.reshape(right_bounds.shape),
    )


def solution(mesh):
    return jax.shard_map(
        local,
        mesh=mesh,
        in_specs=(
            P(("grp", "row"), "col", None, None, None),
            P(("grp", "row"), "col", None, None, None),
            P(("grp", "row"), "col", None, None),
            P(("grp", "row"), "col"),
            P(("grp", "col"), None, None, None),
            P(("grp", "col"), None, None, None),
            P(),
        ),
        out_specs=(
            P(("grp", "row"), "col", None, None),
            P(("grp", "row"), "col", None, None, None),
            P(("grp", "row"), "col", None, None, None),
        ),
        check_vma=False,
    )
```
